512 devices in a mesh: req: 64 (over z, x, core), mdl: 8 (over y).
Axes of the slice: x: 4, y: 8, z: 8, core: 2. Of those that a mesh axis runs over, the one named last changes fastest.
Arguments:
- hidden_in: bfloat16 [8192, 2048], P('req'), may hold values from -6 to 6
- z_weight: bfloat16 [2048, 4096], P('req', 'mdl'), may hold values from -0.125 to 0.125
- x_weight: bfloat16 [2048, 4096], P('req', 'mdl'), may hold values from -0.125 to 0.125
- state_proj: bfloat16 [2048, 256], P('req'), may hold values from -0.125 to 0.125
- step_weight: bfloat16 [2048, 64], P('req', 'mdl'), may hold values from -0.125 to 0.125
- step_bias: float32 [64], P('mdl'), may hold values from -4 to -1
- decay_log: float32 [64], P('mdl'), may hold values from -2 to 1
- skip_gain: float32 [64], P('mdl'), may hold values from 0.5 to 2
- conv_inner: float32 [4, 4096], P(None, 'mdl'), may hold values from -3 to 3
- conv_state: float32 [4, 256], replicated, may hold values from -3 to 3
- norm_gain: float32 [4096], P('mdl'), may hold values from 0.1 to 1.9
- out_weight: bfloat16 [4096, 2048], P('mdl', 'req'), may hold values from -0.09375 to 0.09375
- state_pool: float32 [512, 64, 64, 128], P('req', 'mdl'), may hold values from -2.4 to 2.4
- conv_pool_inner: bfloat16 [512, 3, 4096], P('req', None, 'mdl'), may hold values from -6 to 6
- conv_pool_state: bfloat16 [512, 3, 256], P('req'), may hold values from -6 to 6
- owner_dev: int32 [512], replicated, may hold values from 0 to 63, as said below
- state_page: int32 [512], replicated, may hold values from 0 to 7, as said below
- conv_page: int32 [512], replicated, may hold values from 0 to 7, as said below
- accepted: int32 [512], replicated, may hold values from 1 to 16
Outputs:
- mixed: bfloat16 [8192, 2048], P('req', 'mdl')
- new_states: float32 [512, 64, 64, 128], P('req', 'mdl')
- conv_inner_out: bfloat16 [512, 3, 4096], P('req', None, 'mdl')
- conv_state_out: bfloat16 [512, 3, 256], P('req')
The draws below stay inside these ranges and needn't reach their ends.
Inputs may be any that keep to these rules, and one draw needn't show every extreme that they name: `owner_dev`: request r of device i = r // 8 has its owner among devices i to i + 7 along req, counted modulo the axis size; among the 8 requests of one device at most 2 name the same owner, and exactly 2 do for one owner; every owner is named by exactly 8 requests in all. `state_page`: the requests of one owner have distinct state slots. `conv_page`: the requests of one owner have distinct convolution pages.
All inputs are finite; a program needn't handle non-finite values.
Results may differ from the reference program's by a relative error of at most 0.0069.
Values may be sent and summed in bfloat16 or wider, within the bound.
A program may use at most 64 MiB of HBM per device.

```python
import jax
import jax.numpy as jnp
from jax import lax

D = 2048
HEADS = 64
HDIM = 64
NSTATE = 128
KCONV = 4
DRAFT = 16
CAP = 2
WINDOW = 8
REQ_DEV = 8
INNER = 4096
REQUESTS = 512
TOKENS = 8192


def slot_order(key):
    return jax.random.permutation(key, REQ_DEV).astype(jnp.int32)


def routing(key):
    groups = REQUESTS // REQ_DEV
    keys = jax.random.split(jax.random.fold_in(key, 11), 5)
    distinct = jax.random.permutation(keys[1], WINDOW).astype(jnp.int32)[:REQ_DEV - CAP + 1]
    offsets = jnp.concatenate([jnp.full((CAP - 1,), distinct[0], jnp.int32), distinct])
    offsets = offsets[jax.random.permutation(keys[2], REQ_DEV)]
    homes = jnp.arange(groups, dtype=jnp.int32)[:, None]
    owners = (homes + offsets[None, :]) % groups
    columns = jnp.arange(REQ_DEV, dtype=jnp.int32)[None, :]
    state_perm = jax.vmap(slot_order)(jax.random.split(keys[3], groups))
    conv_perm = jax.vmap(slot_order)(jax.random.split(keys[4], groups))
    state_pages = state_perm[owners, columns]
    conv_pages = conv_perm[owners, columns]
    return (owners.reshape(-1).astype(jnp.int32), state_pages.reshape(-1).astype(jnp.int32), conv_pages.reshape(-1).astype(jnp.int32))


def draw_owner_dev(key, part):
    return routing(key)[0]


def draw_state_page(key, part):
    return routing(key)[1]


def draw_conv_page(key, part):
    return routing(key)[2]


def touch_ends(values, own_key, low, high):
    shape = values.shape
    spot = [jax.random.randint(jax.random.fold_in(own_key, axis), (), 0, shape[axis]) for axis in range(len(shape))]
    values = values.at[tuple(spot)].set(low)
    longest = shape.index(max(shape))
    spot[longest] = (spot[longest] + 1) % shape[longest]
    return values.at[tuple(spot)].set(high)


def block_levels(own_key, shape, pieces, low, largest):
    gain, own = 1.0, jax.random.fold_in(own_key, 6)
    for dim, shards_of in pieces:
        heights = jnp.exp(jax.random.uniform(jax.random.fold_in(own, dim), (shards_of,), jnp.float32, low / len(pieces), largest / len(pieces)))
        gain = gain * jnp.repeat(heights, shape[dim] // shards_of).reshape([-1 if axis == dim else 1 for axis in range(len(shape))])
    return gain


def bell_draw(stream_key, dims, deviation, bound, shards=(), kind=jnp.bfloat16):
    level = block_levels(stream_key, dims, shards, -0.22, 0.18) if shards else 1.0
    result = jax.random.normal(stream_key, dims, jnp.float32) * deviation * level
    return jnp.minimum(jnp.maximum(result, -bound), bound).astype(kind)


def setup_inputs(seed: int = 0) -> dict:
    key_list = jax.random.split(jax.random.key(seed), 20)
    return {
        "hidden_in": bell_draw(key_list[0], (TOKENS, D), 1.0, 6.0, ((0, 64),)),
        "z_weight": bell_draw(key_list[1], (D, INNER), D ** -0.5, 0.125, ((0, 64), (1, 8))),
        "x_weight": bell_draw(key_list[2], (D, INNER), D ** -0.5, 0.125, ((0, 64), (1, 8))),
        "state_proj": bell_draw(key_list[3], (D, 2 * NSTATE), D ** -0.5, 0.125, ((0, 64),)),
        "step_weight": bell_draw(key_list[4], (D, HEADS), D ** -0.5, 0.125, ((0, 64), (1, 8))),
        "step_bias": jnp.clip(-4.0 + 3.0 * jax.random.uniform(key_list[5], (HEADS,), jnp.float32) ** block_levels(key_list[5], (HEADS,), ((0, 8),), -0.2, 0.2), -4.0, -1.0),
        "decay_log": jnp.clip(-2.0 + 3.0 * jax.random.uniform(key_list[6], (HEADS,), jnp.float32) ** block_levels(key_list[6], (HEADS,), ((0, 8),), -0.2, 0.2), -2.0, 1.0),
        "skip_gain": jnp.clip(0.5 + 1.5 * jax.random.uniform(key_list[7], (HEADS,), jnp.float32) ** block_levels(key_list[7], (HEADS,), ((0, 8),), -0.2, 0.2), 0.5, 2.0),
        "conv_inner": bell_draw(key_list[8], (KCONV, INNER), KCONV ** -0.5, 3.0, ((1, 8),), jnp.float32),
        "conv_state": bell_draw(key_list[9], (KCONV, 2 * NSTATE), KCONV ** -0.5, 3.0, (), jnp.float32),
        "norm_gain": jnp.clip(1.0 + 0.18 * jax.random.normal(key_list[10], (INNER,), jnp.float32), 0.1, 1.9),
        "out_weight": bell_draw(key_list[11], (INNER, D), INNER ** -0.5, 0.09375, ((0, 8), (1, 64))),
        "state_pool": bell_draw(key_list[12], (REQUESTS, HEADS, HDIM, NSTATE), 0.3, 2.4, ((0, 64), (1, 8)), jnp.float32),
        "conv_pool_inner": bell_draw(key_list[13], (REQUESTS, KCONV - 1, INNER), 1.0, 6.0, ((0, 64), (2, 8))),
        "conv_pool_state": bell_draw(key_list[14], (REQUESTS, KCONV - 1, 2 * NSTATE), 1.0, 6.0, ((0, 64),)),
        "owner_dev": draw_owner_dev(jax.random.fold_in(key_list[19], 71), 0),
        "state_page": draw_state_page(jax.random.fold_in(key_list[19], 71), 0),
        "conv_page": draw_conv_page(jax.random.fold_in(key_list[19], 71), 0),
        "accepted": touch_ends(jax.random.randint(key_list[18], (REQUESTS,), 1, DRAFT + 1), jax.random.fold_in(key_list[18], 1), 1, DRAFT).astype(jnp.int32),
    }


HIGH = lax.Precision.HIGHEST
EPSILON = 1e-05

def reference(hidden_in, z_weight, x_weight, state_proj, step_weight, step_bias, decay_log, skip_gain, conv_inner, conv_state, norm_gain, out_weight, state_pool, conv_pool_inner, conv_pool_state, owner_dev, state_page, conv_page, accepted):
    gate_pre = jnp.dot(hidden_in, z_weight, preferred_element_type=jnp.float32)
    inner_raw = jnp.dot(hidden_in, x_weight, preferred_element_type=jnp.float32).astype(jnp.bfloat16)
    state_raw = jnp.dot(hidden_in, state_proj, preferred_element_type=jnp.float32).astype(jnp.bfloat16)
    step_raw = jnp.dot(hidden_in, step_weight, preferred_element_type=jnp.float32).astype(jnp.bfloat16)
    packed = jnp.concatenate([inner_raw, state_raw], axis=1).reshape(REQUESTS, DRAFT, INNER + 2 * NSTATE)
    step_rows = step_raw.reshape(REQUESTS, DRAFT, HEADS)
    history = jnp.concatenate([conv_pool_inner, conv_pool_state], axis=2)
    kernel = jnp.concatenate([conv_inner, conv_state], axis=1)
    state_slot = (owner_dev * REQ_DEV + state_page).astype(jnp.int32)
    conv_slot = (owner_dev * REQ_DEV + conv_page).astype(jnp.int32)
    rate = -jnp.exp(decay_log)

    def one_request(item):
        rows, step_in, slot_state, slot_conv, kept_count = item
        series = jnp.concatenate([history[slot_conv], rows], axis=0)
        series_f = series.astype(jnp.float32)
        conv_sum = kernel[0] * series_f[0:DRAFT]
        for tap in range(1, KCONV):
            conv_sum = conv_sum + kernel[tap] * series_f[tap:tap + DRAFT]
        active = jax.nn.silu(conv_sum)
        inputs_x = active[:, :INNER].reshape(DRAFT, HEADS, HDIM)
        b_rows = active[:, INNER:INNER + NSTATE]
        c_rows = active[:, INNER + NSTATE:]
        step_size = jax.nn.softplus(step_in.astype(jnp.float32) + step_bias)
        decay = jnp.exp(step_size * rate)
        start_state = state_pool[slot_state]

        def advance(carry, inputs):
            state_now, chosen = carry
            x_row, b_row, c_row, size_row, decay_row, index_now = inputs
            state_now = decay_row[:, None, None] * state_now + (size_row[:, None] * x_row)[:, :, None] * b_row[None, None, :]
            y_row = jnp.einsum('hpn,n->hp', state_now, c_row, precision=HIGH) + skip_gain[:, None] * x_row
            chosen = jnp.where(index_now + 1 == kept_count, state_now, chosen)
            return ((state_now, chosen), y_row)
        steps_index = jnp.arange(DRAFT, dtype=jnp.int32)
        (final_state, chosen), y_rows = lax.scan(advance, (start_state, jnp.zeros_like(start_state)), (inputs_x, b_rows, c_rows, step_size, decay, steps_index))
        edge_rows = lax.dynamic_slice_in_dim(series, kept_count.astype(jnp.int32), KCONV - 1, 0)
        return (y_rows.reshape(DRAFT, INNER).astype(jnp.bfloat16), chosen, edge_rows)
    mixed_inner, chosen_all, edges_all = lax.map(one_request, (packed, step_rows, state_slot, conv_slot, accepted))
    gated = mixed_inner.reshape(TOKENS, INNER).astype(jnp.float32) * jax.nn.silu(gate_pre)
    mean_square = lax.optimization_barrier(jnp.mean(gated * gated, axis=1, keepdims=True))
    normed = (gated * lax.rsqrt(mean_square + EPSILON) * norm_gain).astype(jnp.bfloat16)
    mixed = jnp.dot(normed, out_weight, preferred_element_type=jnp.float32).astype(jnp.bfloat16)
    new_states = jnp.zeros_like(state_pool).at[state_slot].set(chosen_all)
    conv_out = jnp.zeros_like(history).at[conv_slot].set(edges_all)
    return (mixed, new_states, conv_out[:, :, :INNER], conv_out[:, :, INNER:])
```

```python
import functools

import jax
import jax.numpy as jnp
from jax import lax
from jax.experimental import pallas as pl
from jax.experimental.pallas import tpu as pltpu
from jax.sharding import PartitionSpec as P

KCONV = 4
CAP = 2
WINDOW = 8
SLOTS = WINDOW * CAP
XN = 4
HIGH = lax.Precision.HIGHEST
EPSILON = 1e-05
MESH = pl.DeviceIdType.MESH
NT = (((1,), (1,)), ((), ()))


def route_tables(owner_dev, state_page, conv_page, accepted, groups, per_dev, this_dev):
    owner_grid = owner_dev.reshape(groups, per_dev)
    home_grid = jnp.arange(groups, dtype=jnp.int32)[:, None]
    offset_grid = (owner_grid - home_grid + groups) % groups
    positions = jnp.arange(per_dev, dtype=jnp.int32)
    earlier = positions[None, :] < positions[:, None]
    pair_rank = jnp.sum((owner_grid[:, :, None] == owner_grid[:, None, :]) & earlier[None], axis=2)
    slot_grid = offset_grid * CAP + pair_rank
    slot_of = lax.dynamic_slice_in_dim(slot_grid, this_dev, 1, 0)[0]
    slot_ids = jnp.arange(SLOTS, dtype=jnp.int32)
    source_of = jnp.sum(
        jnp.where(slot_ids[:, None] == slot_of[None, :], positions[None, :], 0), axis=1
    )
    arrive_at = slot_grid.reshape(-1)
    match = (owner_dev[None, :] == this_dev) & (state_page[None, :] == positions[:, None])
    pick_from = jnp.sum(jnp.where(match, arrive_at[None, :], 0), axis=1)
    conv_of = jnp.sum(jnp.where(match, conv_page[None, :], 0), axis=1)
    kept_count = jnp.sum(jnp.where(match, accepted[None, :], 0), axis=1)
    page_of = jnp.sum(
        jnp.where(slot_ids[:, None] == pick_from[None, :], positions[None, :], 0), axis=1
    )
    return slot_of, source_of, pick_from, page_of, conv_of, kept_count


def greet(peers):
    barrier = pltpu.get_barrier_semaphore()
    for peer in peers:
        pl.semaphore_signal(barrier, inc=1, device_id=peer, device_id_type=MESH)
    pl.semaphore_wait(barrier, len(peers))


class Copies:
    def __init__(self, send_sem, recv_sem):
        self.send_sem, self.recv_sem = send_sem, recv_sem
        self.keys, self.started = {}, []

    def key(self, name):
        return self.keys.setdefault(name, len(self.keys))

    def send(self, name, src, dst, peer):
        k = self.key(name)
        copy = pltpu.make_async_remote_copy(
            src_ref=src,
            dst_ref=dst,
            send_sem=self.send_sem.at[k],
            recv_sem=self.recv_sem.at[k],
            device_id=peer,
            device_id_type=MESH,
        )
        copy.start()
        self.started.append(copy)

    def arrive(self, name, where, peer):
        k = self.key(name)
        pltpu.make_async_remote_copy(
            src_ref=where,
            dst_ref=where,
            send_sem=self.send_sem.at[k],
            recv_sem=self.recv_sem.at[k],
            device_id=peer,
            device_id_type=MESH,
        ).wait_recv()

    def finish(self):
        for copy in self.started:
            copy.wait_send()


def gather_kernel(
    groups,
    mdl_size,
    source_of,
    pick_from,
    hidden,
    shard,
    full,
    rows_full,
    outgoing,
    incoming,
    owned,
    send_sem,
    recv_sem,
    own_sem,
):
    zn = groups // (2 * XN)
    me = lax.axis_index("req")
    col = lax.axis_index("mdl")
    core = me % 2
    x = (me // 2) % XN
    z = me // (2 * XN)
    width = hidden.shape[2] // mdl_size

    def at(zz, xx, cc):
        return {"req": ((zz + zn) % zn * XN + (xx + XN) % XN) * 2 + cc}

    def zi(v):
        return (v + zn) % zn

    def xi(v):
        return (v + XN) % XN

    sibling = {"req": me + 1 - 2 * core}
    up, down = at(z + 1, x, core), at(z - 1, x, core)
    xs = [at(z, x + d, core) for d in range(1, XN)]
    ahead = [{"req": (me + o) % groups} for o in range(1, WINDOW)]
    behind = [{"req": (me - o + groups) % groups} for o in range(1, WINDOW)]
    across = [{"mdl": (col + k) % mdl_size} for k in range(1, mdl_size)]
    greet([sibling, up, down] + xs + ahead + behind + across)

    copies = Copies(send_sem, recv_sem)
    half_up = zn // 2
    half_down = (zn - 1) // 2
    split_z = zn % 2 == 0
    hx = XN // 2

    own = pltpu.make_async_copy(shard, full.at[z, x, core], own_sem.at[0])
    own.start()
    for d in range(1, XN):
        copies.send(("ax", d), shard.at[0], full.at[z, x, core, 0], xs[d - 1])
    copies.send(("bu", 1), shard.at[1], full.at[z, x, core, 1], up)
    copies.send(("bd", 1), shard.at[1], full.at[z, x, core, 1], down)

    for s in range(SLOTS):
        outgoing[s] = hidden[source_of[s], :, pl.ds(pl.multiple_of(col * width, width), width)]
    for o in range(1, WINDOW):
        part = pl.ds(o * CAP, CAP)
        copies.send(("h", o), outgoing.at[part], incoming.at[part], ahead[o - 1])
    incoming[0:CAP] = outgoing[0:CAP]

    for s in range(1, half_up + 1):
        piece = full.at[zi(z - s), x, core, 1]
        copies.arrive(("bu", s), piece, up)
        if s < half_up:
            copies.send(("bu", s + 1), piece, piece, up)
        if s <= half_down:
            piece = full.at[zi(z + s), x, core, 1]
            copies.arrive(("bd", s), piece, up)
            if s < half_down:
                copies.send(("bd", s + 1), piece, piece, down)
        if s == 1:
            own.wait()
            for d in range(1, XN):
                copies.arrive(("ax", d), full.at[z, xi(x - d), core, 0], up)
            block = full.at[z, :, core, 0]
            copies.send(("au", 1), block, block, up)
            copies.send(("ad", 1), block, block, down)
            copies.send(("sa", 0), block, block, sibling)
    line = full.at[:, x, core, 1]
    copies.send(("bx", 1), line, line, at(z, x + 1, core))
    copies.send(("bx", 3), line, line, at(z, x - 1, core))
    copies.send(("sb", 0), line, line, sibling)

    for o in range(1, WINDOW):
        copies.arrive(("h", o), incoming.at[pl.ds(o * CAP, CAP)], up)
    for p in range(hidden.shape[0]):
        owned[p] = incoming[pick_from[p]]
    keep = pltpu.make_async_copy(owned, rows_full.at[col], own_sem.at[1])
    keep.start()
    for k in range(1, mdl_size):
        copies.send(("y", k), owned, rows_full.at[col], across[k - 1])

    def forward_x():
        back, front = full.at[:, xi(x - 1), core, 1], full.at[:, xi(x + 1), core, 1]
        copies.arrive(("bx", 1), back, up)
        copies.arrive(("bx", 3), front, up)
        low, high = pl.ds(0, half_up), pl.ds(half_up, zn - half_up)
        a = full.at[low, xi(x - 1), core, 1]
        b = full.at[high, xi(x + 1), core, 1]
        copies.send(("bx", 2), a, a, at(z, x + 1, core))
        copies.send(("bx", 4), b, b, at(z, x - 1, core))
        copies.send(("sb", 1), back, back, sibling)
        copies.send(("sb", 3), front, front, sibling)

    for s in range(1, half_up + 1):
        last = split_z and s == half_up
        xu = pl.ds(0, hx) if last else pl.ds(0, XN)
        xd = pl.ds(hx, XN - hx) if last else pl.ds(0, XN)
        bu = full.at[zi(z - s), xu, core, 0]
        bd = full.at[zi(z + s), xd, core, 0]
        copies.arrive(("au", s), bu, up)
        if s < half_up:
            nu = pl.ds(0, hx) if split_z and s + 1 == half_up else xu
            piece = full.at[zi(z - s), nu, core, 0]
            copies.send(("au", s + 1), piece, piece, up)
        copies.arrive(("ad", s), bd, up)
        if s < half_up:
            nd = pl.ds(hx, XN - hx) if split_z and s + 1 == half_up else xd
            piece = full.at[zi(z + s), nd, core, 0]
            copies.send(("ad", s + 1), piece, piece, down)
        copies.send(("sau", s), bu, bu, sibling)
        copies.send(("sad", s), bd, bd, sibling)
        if s == half_up - 1:
            forward_x()

    far = xi(x + 2)
    low, high = pl.ds(0, half_up), pl.ds(half_up, zn - half_up)
    copies.arrive(("bx", 2), full.at[low, far, core, 1], up)
    copies.arrive(("bx", 4), full.at[high, far, core, 1], up)
    rest = full.at[:, far, core, 1]
    copies.send(("sb", 2), rest, rest, sibling)

    other = 1 - core
    copies.arrive(("sa", 0), full.at[z, :, other, 0], up)
    for j in range(XN):
        copies.arrive(("sb", j), full.at[:, xi(x - j), other, 1], up)
    for s in range(1, half_up + 1):
        last = split_z and s == half_up
        xu = pl.ds(0, hx) if last else pl.ds(0, XN)
        xd = pl.ds(hx, XN - hx) if last else pl.ds(0, XN)
        copies.arrive(("sau", s), full.at[zi(z - s), xu, other, 0], up)
        copies.arrive(("sad", s), full.at[zi(z + s), xd, other, 0], up)
    for k in range(1, mdl_size):
        copies.arrive(("y", k), rows_full.at[(col - k + mdl_size) % mdl_size], up)
    keep.wait()
    copies.finish()


def gather(source_of, pick_from, hidden, shard, groups, mdl_size):
    per_dev, draft, depth = hidden.shape
    zn = groups // (2 * XN)
    width = depth // mdl_size
    count = 96
    return pl.pallas_call(
        functools.partial(gather_kernel, groups, mdl_size),
        out_shape=(
            jax.ShapeDtypeStruct((zn, XN, 2) + shard.shape, shard.dtype),
            jax.ShapeDtypeStruct((mdl_size, per_dev, draft, width), hidden.dtype),
        ),
        in_specs=[
            pl.BlockSpec(memory_space=pltpu.SMEM),
            pl.BlockSpec(memory_space=pltpu.SMEM),
            pl.BlockSpec(memory_space=pltpu.VMEM),
            pl.BlockSpec(memory_space=pl.ANY),
        ],
        out_specs=(
            pl.BlockSpec(memory_space=pl.ANY),
            pl.BlockSpec(memory_space=pl.ANY),
        ),
        scratch_shapes=[
            pltpu.VMEM((SLOTS, draft, width), hidden.dtype),
            pltpu.VMEM((SLOTS, draft, width), hidden.dtype),
            pltpu.VMEM((per_dev, draft, width), hidden.dtype),
            pltpu.SemaphoreType.DMA((count,)),
            pltpu.SemaphoreType.DMA((count,)),
            pltpu.SemaphoreType.DMA((2,)),
        ],
        compiler_params=pltpu.CompilerParams(collective_id=0, has_side_effects=True),
        name="gather_rows_and_weights",
    )(source_of, pick_from, hidden, shard)


def dot(a, b, precision=None):
    return jnp.dot(a, b, preferred_element_type=jnp.float32, precision=precision)


def dot_nt(a, b, precision=None):
    return lax.dot_general(a, b, NT, preferred_element_type=jnp.float32, precision=precision)


def mix_kernel(
    dims,
    conv_of,
    kept,
    step_bias,
    decay_log,
    skip_gain,
    rows_full,
    weights,
    conv_inner,
    conv_state,
    norm_gain,
    state_pool,
    hist_inner,
    hist_state,
    terms,
    squares,
    new_states,
    edge_inner,
    edge_state,
    acc,
    out_t,
    series_x,
    series_s,
    hist_x,
    hist_s,
    edge_x,
    edge_s,
    carried,
):
    per_dev, draft, heads, hdim, nstate, inner, columns = dims
    step = pl.program_id(0)
    depth = weights.shape[0]
    tokens = per_dev * draft
    wide = 2 * inner + 2 * nstate + 128
    blk = rows_full[...].reshape(tokens, depth)
    part = dot(blk, weights[:, :wide])
    out_t[pl.ds(pl.multiple_of(step * depth, depth), depth), :] = weights[:, wide:]

    @pl.when(step == 0)
    def _():
        acc[...] = part

    @pl.when(step > 0)
    def _():
        acc[...] += part

    @pl.when(step == pl.num_programs(0) - 1)
    def _():
        f32, bf16 = jnp.float32, jnp.bfloat16
        hist_x[...] = hist_inner[...].astype(f32)
        hist_s[...] = hist_state[...].astype(f32)
        x_raw = acc[:, inner : 2 * inner].astype(bf16).astype(f32)
        s_raw = acc[:, 2 * inner : 2 * inner + 2 * nstate].astype(bf16).astype(f32)
        series_x[:, 8:, :] = x_raw.reshape(per_dev, draft, inner)
        series_s[:, 8:, :] = s_raw.reshape(per_dev, draft, 2 * nstate)
        lead = 8 - (KCONV - 1)
        for p in range(per_dev):
            for j in range(KCONV - 1):
                series_x[p, lead + j : lead + j + 1, :] = hist_x[j, pl.ds(conv_of[p], 1), :]
                series_s[p, lead + j : lead + j + 1, :] = hist_s[j, pl.ds(conv_of[p], 1), :]
        for p in range(per_dev):
            for j in range(KCONV - 1):
                edge_x[j, pl.ds(conv_of[p], 1), :] = series_x[p, pl.ds(lead + kept[p] + j, 1), :]
                edge_s[j, pl.ds(conv_of[p], 1), :] = series_s[p, pl.ds(lead + kept[p] + j, 1), :]
        edge_inner[...] = edge_x[...].astype(bf16)
        edge_state[...] = edge_s[...].astype(bf16)

        def conv(series, taps):
            total = taps[0:1, :] * series[:, lead : lead + draft, :]
            for k in range(1, KCONV):
                total = total + taps[k : k + 1, :] * series[:, lead + k : lead + k + draft, :]
            return jax.nn.silu(total).reshape(tokens, total.shape[2])

        active = conv(series_x, conv_inner)
        maps = conv(series_s, conv_state)
        b_rows, c_rows = maps[:, :nstate], maps[:, nstate:]

        lane = lax.broadcasted_iota(jnp.int32, (1, 128), 1)
        bias_row = jnp.zeros((1, 128), f32)
        rate_row = jnp.zeros((1, 128), f32)
        for h in range(heads):
            bias_row = jnp.where(lane == h, step_bias[h], bias_row)
            rate_row = jnp.where(lane == h, decay_log[h], rate_row)
        rate_row = jnp.exp(rate_row)
        step_raw = acc[:, 2 * inner + 2 * nstate : wide].astype(bf16).astype(f32)
        size = jax.nn.softplus(step_raw + bias_row)
        rows_i = lax.broadcasted_iota(jnp.int32, (tokens, tokens), 0)
        cols_i = lax.broadcasted_iota(jnp.int32, (tokens, tokens), 1)
        causal = (rows_i // draft == cols_i // draft) & (cols_i <= rows_i)
        decay = dot(causal.astype(f32), -size * rate_row, HIGH)
        decay_t, size_t = decay.T, size.T
        scores = dot_nt(c_rows, b_rows, HIGH)

        end_at = jnp.zeros((tokens, tokens), jnp.int32)
        for p in range(per_dev):
            end_at = jnp.where(rows_i // draft == p, p * draft + kept[p] - 1, end_at)
        end_decay = dot((cols_i == end_at).astype(f32), decay, HIGH)
        before = rows_i <= end_at
        chosen_w = jnp.where(before, jnp.exp(jnp.where(before, end_decay - decay, 0.0)), 0.0) * size
        grown = jnp.exp(decay)
        end_grown = jnp.exp(end_decay)

        b_low = b_rows.astype(bf16)
        c_low = c_rows.astype(bf16)
        for p in range(per_dev):
            start = state_pool[p].reshape(inner, nstate)
            carried[p * draft : (p + 1) * draft, :] = dot_nt(
                c_low[p * draft : (p + 1) * draft, :], start.astype(bf16)
            )

        left = lax.broadcasted_iota(jnp.int32, (tokens, 128), 1) < hdim

        def spread(table, j):
            return jnp.where(left, table[:, 2 * j : 2 * j + 1], table[:, 2 * j + 1 : 2 * j + 2])

        total = jnp.zeros((tokens, 128), f32)
        gated_cols = []
        picked_t = []
        for j in range(heads // 2):
            cols = slice(j * 128, (j + 1) * 128)
            x_pair = active[:, cols]
            x_low = x_pair.astype(bf16)
            halves = []
            for h in (2 * j, 2 * j + 1):
                gap = decay[:, h : h + 1] - decay_t[h : h + 1, :]
                weight = jnp.exp(jnp.where(causal, gap, -1e30)) * scores * size_t[h : h + 1, :]
                halves.append(dot(weight.astype(bf16), x_low))
            skip = jnp.where(left, skip_gain[2 * j], skip_gain[2 * j + 1])
            y = (
                jnp.where(left, halves[0], halves[1])
                + carried[:, cols] * spread(grown, j)
                + skip * x_pair
            )
            gate = jax.nn.silu(acc[:, cols])
            gated = y.astype(bf16).astype(f32) * gate
            total = total + gated * gated
            gated_cols.append((gated * norm_gain[0:1, cols]).astype(bf16))
            picked_t.append((x_pair * spread(chosen_w, j)).T.astype(bf16))
        gated_low = jnp.concatenate(gated_cols, axis=1)
        squares[...] = dot_nt(jnp.ones((8, 128), f32), total, HIGH)
        piece = out_t.shape[0] // terms.shape[0]
        for m in range(terms.shape[0]):
            terms[m] = dot_nt(gated_low, out_t[m * piece : (m + 1) * piece, :]).astype(bf16)

        picked = jnp.concatenate(picked_t, axis=0)
        row_of = lax.broadcasted_iota(jnp.int32, (tokens, nstate), 0) // draft
        for p in range(per_dev):
            masked = jnp.where(row_of == p, b_low, jnp.zeros_like(b_low))
            added = dot(picked, masked)
            for h in range(heads):
                factor = end_grown[p * draft : p * draft + 1, h : h + 1]
                new_states[p, h] = factor * state_pool[p, h] + added[h * hdim : (h + 1) * hdim, :]


def mix(
    conv_of,
    kept,
    step_bias,
    decay_log,
    skip_gain,
    rows_full,
    weights,
    conv_inner,
    conv_state,
    norm_gain,
    state_pool,
    hist_inner,
    hist_state,
):
    mdl_size, per_dev, draft, width = rows_full.shape
    _, heads, hdim, nstate = state_pool.shape
    depth, packed = weights.shape
    inner = heads * hdim
    tokens = per_dev * draft
    columns = depth
    smem = pl.BlockSpec(memory_space=pltpu.SMEM)

    def whole(a):
        return pl.BlockSpec(
            a.shape, lambda k: (0,) * len(a.shape), pipeline_mode=pl.Buffered(1)
        )

    out_shape = (
        jax.ShapeDtypeStruct((mdl_size, tokens, columns // mdl_size), jnp.bfloat16),
        jax.ShapeDtypeStruct((8, tokens), jnp.float32),
        jax.ShapeDtypeStruct(state_pool.shape, state_pool.dtype),
        jax.ShapeDtypeStruct(hist_inner.shape, hist_inner.dtype),
        jax.ShapeDtypeStruct(hist_state.shape, hist_state.dtype),
    )
    f32 = jnp.float32
    return pl.pallas_call(
        functools.partial(mix_kernel, (per_dev, draft, heads, hdim, nstate, inner, columns)),
        grid=(mdl_size,),
        out_shape=out_shape,
        in_specs=[smem] * 5
        + [
            pl.BlockSpec((None, per_dev, draft, width), lambda k: (k, 0, 0, 0)),
            pl.BlockSpec((width, packed), lambda k: (k, 0)),
        ]
        + [
            whole(a)
            for a in (conv_inner, conv_state, norm_gain, state_pool, hist_inner, hist_state)
        ],
        out_specs=tuple(whole(o) for o in out_shape),
        scratch_shapes=[
            pltpu.VMEM((tokens, 2 * inner + 2 * nstate + 128), f32),
            pltpu.VMEM((depth, inner), jnp.bfloat16),
            pltpu.VMEM((per_dev, draft + 8, inner), f32),
            pltpu.VMEM((per_dev, draft + 8, 2 * nstate), f32),
            pltpu.VMEM((KCONV - 1, per_dev, inner), f32),
            pltpu.VMEM((KCONV - 1, per_dev, 2 * nstate), f32),
            pltpu.VMEM((KCONV - 1, per_dev, inner), f32),
            pltpu.VMEM((KCONV - 1, per_dev, 2 * nstate), f32),
            pltpu.VMEM((tokens, inner), f32),
        ],
        compiler_params=pltpu.CompilerParams(vmem_limit_bytes=40 << 20),
        name="project_and_mix",
    )(
        conv_of,
        kept,
        step_bias,
        decay_log,
        skip_gain,
        rows_full,
        weights,
        conv_inner,
        conv_state,
        norm_gain,
        state_pool,
        hist_inner,
        hist_state,
    )


def return_kernel(
    groups,
    mdl_size,
    page_of,
    slot_of,
    terms,
    squares,
    mixed,
    parts,
    square_parts,
    result,
    outgoing,
    incoming,
    send_sem,
    recv_sem,
):
    me = lax.axis_index("req")
    col = lax.axis_index("mdl")
    per_dev, draft, columns = mixed.shape
    tokens = per_dev * draft
    ahead = [{"req": (me + o) % groups} for o in range(1, WINDOW)]
    behind = [{"req": (me - o + groups) % groups} for o in range(1, WINDOW)]
    across = [{"mdl": (col + k) % mdl_size} for k in range(1, mdl_size)]
    greet(ahead + behind + across)
    copies = Copies(send_sem, recv_sem)
    for k in range(1, mdl_size):
        copies.send(("s", k), squares, square_parts.at[k], across[k - 1])
    for k in sorted(range(1, mdl_size), key=lambda k: -min(k, mdl_size - k)):
        copies.send(("t", k), terms.at[(col + k) % mdl_size], parts.at[k], across[k - 1])
    square_parts[0] = squares[...]
    total = terms[col].astype(jnp.float32)
    for k in range(1, mdl_size):
        copies.arrive(("s", k), square_parts.at[k], across[0])
    stacked = square_parts[...].reshape(mdl_size * 8, tokens)
    ones = jnp.full((mdl_size * 8, columns), 0.125, jnp.float32)
    mean = lax.dot_general(
        stacked,
        ones,
        (((0,), (0,)), ((), ())),
        preferred_element_type=jnp.float32,
        precision=HIGH,
    ) / (mdl_size * 512)
    scale = lax.rsqrt(mean + EPSILON)
    for k in sorted(range(1, mdl_size), key=lambda k: min(k, mdl_size - k)):
        copies.arrive(("t", k), parts.at[k], across[0])
        total = total + parts[k].astype(jnp.float32)
    result[...] = (total * scale).astype(jnp.bfloat16).reshape(per_dev, draft, columns)
    for s in range(SLOTS):
        outgoing[s] = result[page_of[s]]
    for o in range(1, WINDOW):
        part = pl.ds(o * CAP, CAP)
        copies.send(("r", o), outgoing.at[part], incoming.at[part], behind[o - 1])
    incoming[0:CAP] = outgoing[0:CAP]
    for o in range(1, WINDOW):
        copies.arrive(("r", o), incoming.at[pl.ds(o * CAP, CAP)], across[0])
    for q in range(per_dev):
        mixed[q] = incoming[slot_of[q]]
    copies.finish()


def give_back(page_of, slot_of, terms, squares, per_dev, groups, mdl_size):
    _, tokens, columns = terms.shape
    draft = tokens // per_dev
    bf16 = jnp.bfloat16
    count = 2 * mdl_size + WINDOW
    vmem = pl.BlockSpec(memory_space=pltpu.VMEM)
    smem = pl.BlockSpec(memory_space=pltpu.SMEM)
    return pl.pallas_call(
        functools.partial(return_kernel, groups, mdl_size),
        out_shape=jax.ShapeDtypeStruct((per_dev, draft, columns), bf16),
        in_specs=[smem, smem, vmem, vmem],
        out_specs=vmem,
        scratch_shapes=[
            pltpu.VMEM((mdl_size, tokens, columns), bf16),
            pltpu.VMEM((mdl_size, 8, tokens), jnp.float32),
            pltpu.VMEM((per_dev, draft, columns), bf16),
            pltpu.VMEM((SLOTS, draft, columns), bf16),
            pltpu.VMEM((SLOTS, draft, columns), bf16),
            pltpu.SemaphoreType.DMA((count,)),
            pltpu.SemaphoreType.DMA((count,)),
        ],
        compiler_params=pltpu.CompilerParams(collective_id=1, has_side_effects=True),
        name="sum_and_return_rows",
    )(page_of, slot_of, terms, squares)


def on_device(
    hidden_in,
    z_weight,
    x_weight,
    state_proj,
    step_weight,
    step_bias,
    decay_log,
    skip_gain,
    conv_inner,
    conv_state,
    norm_gain,
    out_weight,
    state_pool,
    conv_pool_inner,
    conv_pool_state,
    owner_dev,
    state_page,
    conv_page,
    accepted,
):
    groups = lax.axis_size("req")
    mdl_size = lax.axis_size("mdl")
    this_dev = lax.axis_index("req")
    per_dev, heads = state_pool.shape[0], state_pool.shape[1]
    tokens, depth = hidden_in.shape
    draft = tokens // per_dev
    slot_of, source_of, pick_from, page_of, conv_of, kept = route_tables(
        owner_dev, state_page, conv_page, accepted, groups, per_dev, this_dev
    )
    shard = jnp.concatenate(
        [
            z_weight,
            x_weight,
            state_proj,
            jnp.pad(step_weight, ((0, 0), (0, 128 - heads))),
            out_weight.T,
        ],
        axis=1,
    )
    rows_shard, packed = shard.shape
    full, rows_full = gather(
        source_of,
        pick_from,
        hidden_in.reshape(per_dev, draft, depth),
        shard.reshape(2, rows_shard // 2, packed),
        groups,
        mdl_size,
    )
    terms, squares, new_states, edge_inner, edge_state = mix(
        conv_of,
        kept,
        step_bias,
        decay_log,
        skip_gain,
        rows_full,
        full.reshape(groups * rows_shard, packed),
        conv_inner,
        conv_state,
        norm_gain.reshape(1, -1),
        state_pool,
        conv_pool_inner.transpose(1, 0, 2),
        conv_pool_state.transpose(1, 0, 2),
    )
    mixed = give_back(page_of, slot_of, terms, squares, per_dev, groups, mdl_size)
    return (
        mixed.reshape(tokens, -1),
        new_states,
        edge_inner.transpose(1, 0, 2),
        edge_state.transpose(1, 0, 2),
    )


def solution(mesh):
    return jax.shard_map(
        on_device,
        mesh=mesh,
        in_specs=(
            P("req", None),
            P("req", "mdl"),
            P("req", "mdl"),
            P("req", None),
            P("req", "mdl"),
            P("mdl"),
            P("mdl"),
            P("mdl"),
            P(None, "mdl"),
            P(),
            P("mdl"),
            P("mdl", "req"),
            P("req", "mdl", None, None),
            P("req", None, "mdl"),
            P("req", None, None),
            P(),
            P(),
            P(),
            P(),
        ),
        out_specs=(
            P("req", "mdl"),
            P("req", "mdl", None, None),
            P("req", None, "mdl"),
            P("req", None, None),
        ),
        check_vma=False,
    )
```

```python
import functools

import jax
import jax.numpy as jnp
from jax import lax
from jax.experimental import pallas as pl
from jax.experimental.pallas import tpu as pltpu
from jax.sharding import PartitionSpec as P

KCONV = 4
CAP = 2
WINDOW = 8
SLOTS = WINDOW * CAP
XN = 4
PAD = 128
HIGH = lax.Precision.HIGHEST
EPSILON = 1e-05
MESH = pl.DeviceIdType.MESH
NT = (((1,), (1,)), ((), ()))
TN = (((0,), (0,)), ((), ()))


def dot(a, b, precision=None):
    return jnp.dot(a, b, preferred_element_type=jnp.float32, precision=precision)


def dot_nt(a, b, precision=None):
    return lax.dot_general(a, b, NT, preferred_element_type=jnp.float32, precision=precision)


class Copies:
    def __init__(self, send_sem, recv_sem, anyone):
        self.send_sem, self.recv_sem, self.anyone = send_sem, recv_sem, anyone
        self.keys, self.groups = {}, {}

    def describe(self, name, group, src, dst, peer):
        k = self.keys.setdefault(name, len(self.keys))
        g = self.groups.setdefault(group, len(self.groups))
        return pltpu.make_async_remote_copy(
            src_ref=src,
            dst_ref=dst,
            send_sem=self.send_sem.at[g],
            recv_sem=self.recv_sem.at[k],
            device_id=peer,
            device_id_type=MESH,
        )

    def send(self, name, group, src, dst, peer):
        self.describe(name, group, src, dst, peer).start()

    def arrive(self, name, group, where):
        self.describe(name, group, where, where, self.anyone).wait_recv()

    def sent(self, group, whole):
        pltpu.make_async_copy(whole, whole, self.send_sem.at[self.groups[group]]).wait()


def layer_kernel(
    groups,
    mdl_size,
    owner_dev,
    state_page,
    conv_page,
    accepted,
    step_bias,
    decay_log,
    skip_gain,
    z_weight,
    x_weight,
    state_proj,
    step_t,
    out_t,
    conv_inner,
    conv_state,
    norm_gain,
    hist_inner,
    hist_state,
    hidden,
    state_pool,
    mixed,
    new_states,
    edge_inner,
    edge_state,
    full_a,
    full_b,
    rows_full,
    slice_in,
    outgoing,
    incoming,
    state,
    acc_a,
    acc_b,
    series_x,
    series_s,
    hist_x,
    hist_s,
    edge_x,
    edge_s,
    carried,
    table,
    decay_s,
    terms,
    squares,
    parts,
    square_parts,
    result,
    outgoing2,
    incoming2,
    send_sem,
    recv_sem,
    local_sem,
):
    f32, bf16 = jnp.float32, jnp.bfloat16
    per_dev, draft, columns = mixed.shape
    tokens = per_dev * draft
    heads, hdim, nstate = state.shape[1:]
    inner = heads * hdim
    width = slice_in.shape[2]
    zn = groups // (2 * XN)
    me = lax.axis_index("req")
    col = lax.axis_index("mdl")
    core = me % 2
    x = (me // 2) % XN
    z = me // (2 * XN)

    def zi(v):
        return (v + zn) % zn

    def xi(v):
        return (v + XN) % XN

    def at(zz, xx):
        return {"req": (zi(zz) * XN + xi(xx)) * 2 + core}

    load_rows = pltpu.make_async_copy(
        hidden.at[:, :, pl.ds(pl.multiple_of(col * width, width), width)],
        slice_in,
        local_sem.at[0],
    )
    load_rows.start()
    load_state = pltpu.make_async_copy(state_pool, state, local_sem.at[1])
    load_state.start()

    sibling = {"req": me + 1 - 2 * core}
    up, down = at(z + 1, x), at(z - 1, x)
    right, left_x = at(z, x + 1), at(z, x - 1)
    xs = [at(z, x + d) for d in range(1, XN)]
    ahead = [{"req": (me + o) % groups} for o in range(1, WINDOW)]
    behind = [{"req": (me - o + groups) % groups} for o in range(1, WINDOW)]
    across = [{"mdl": (col + k) % mdl_size} for k in range(1, mdl_size)]
    peers = [sibling, up, down] + xs + ahead + behind + across
    barrier = pltpu.get_barrier_semaphore()
    for peer in peers:
        pl.semaphore_signal(barrier, inc=1, device_id=peer, device_id_type=MESH)

    full_a[z, x, core, :, :inner] = z_weight[...]
    full_a[z, x, core, :, inner:] = state_proj[...]
    full_b[z, x, core, :, :inner] = x_weight[...]
    place = (
        lax.broadcasted_iota(jnp.int32, (heads, PAD), 0)
        == lax.broadcasted_iota(jnp.int32, (heads, PAD), 1)
    ).astype(f32)
    full_b[z, x, core, :, inner : inner + PAD] = lax.dot_general(
        step_t[...].astype(f32), place, TN, preferred_element_type=f32, precision=HIGH
    ).astype(bf16)
    full_b[z, x, core, :, inner + PAD :] = out_t[...]
    pl.semaphore_wait(barrier, len(peers))

    copies = Copies(send_sem, recv_sem, up)
    half = zn // 2
    rows = full_a.shape[3]
    halves = (pl.ds(0, rows // 2), pl.ds(rows // 2, rows // 2))
    order = [0]
    for s in range(1, half):
        order += [-s, s]
    order.append(-half)
    place_of = {d: n for n, d in enumerate(order)}

    def piece_a(dz, dx):
        return full_a.at[zi(z + dz), xi(x + dx), core]

    def piece_b(dz, dx):
        return full_b.at[zi(z + dz), xi(x + dx), core]

    def a_up(s, d):
        group = "a_last" if s == half else "a"
        copies.send(("au", s, d), group, piece_a(1 - s, -d), piece_a(1 - s, -d), up)

    def a_down(s, d):
        group = "a_last" if s == half else "a"
        copies.send(("ad", s, d), group, piece_a(s - 1, -d), piece_a(s - 1, -d), down)

    up_last, down_last = range(0, XN // 2), range(XN // 2, XN)

    def b_up(s):
        p = piece_b(1 - s, 0)
        if s == half:
            copies.send(("bu", s), "b_last", p.at[halves[0]], p.at[halves[0]], up)
        else:
            copies.send(("bu", s), "b", p, p, up)

    def b_down(s):
        p = piece_b(s - 1, 0)
        if s == half:
            copies.send(("bd", s), "b_last", p.at[halves[1]], p.at[halves[1]], down)
        else:
            copies.send(("bd", s), "b", p, p, down)

    def b_side(n):
        p = piece_b(order[n], 0)
        copies.send(("br", n), "bx", p, p, right)
        copies.send(("bl", n), "bx", p, p, left_x)

    def e_ax(d):
        copies.arrive(("ax", d), "ax", piece_a(0, -d))
        a_up(1, d)
        a_down(1, d)

    def e_bz(s):
        if s < half:
            copies.arrive(("bu", s), "b", piece_b(-s, 0))
            b_up(s + 1)
            b_side(place_of[-s])
            copies.arrive(("bd", s), "b", piece_b(s, 0))
            b_down(s + 1)
            b_side(place_of[s])
        else:
            copies.arrive(("bu", s), "b_last", piece_b(-s, 0).at[halves[0]])
            copies.arrive(("bd", s), "b_last", piece_b(-s, 0).at[halves[1]])
            b_side(place_of[-s])

    def e_a(s, d):
        if s < half:
            copies.arrive(("au", s, d), "a", piece_a(-s, -d))
            if s + 1 < half or d in up_last:
                a_up(s + 1, d)
            copies.arrive(("ad", s, d), "a", piece_a(s, -d))
            if s + 1 < half or d in down_last:
                a_down(s + 1, d)
        elif d in up_last:
            copies.arrive(("au", s, d), "a_last", piece_a(-s, -d))
        else:
            copies.arrive(("ad", s, d), "a_last", piece_a(-s, -d))

    def e_bx(n):
        copies.arrive(("br", n), "bx", piece_b(order[n], -1))
        copies.arrive(("bl", n), "bx", piece_b(order[n], 1))
        if n % 2 == 0:
            p = piece_b(order[n], -1)
            copies.send(("bf", n), "bf", p, p, right)
        else:
            p = piece_b(order[n], 1)
            copies.send(("bf", n), "bf", p, p, left_x)

    def e_bf(n):
        copies.arrive(("bf", n), "bf", piece_b(order[n], 2))

    def e_sib(n):
        a = full_a.at[zi(z + order[n]), :, core]
        b = full_b.at[zi(z + order[n]), :, core]
        copies.send(("sa", n), "sa", a, a, sibling)
        copies.send(("sb", n), "sb", b, b, sibling)

    def e_proj(n):
        zz = zi(z + order[n])
        copies.arrive(("sa", n), "sa", full_a.at[zz, :, 1 - core])
        copies.arrive(("sb", n), "sb", full_b.at[zz, :, 1 - core])
        blk = rows_full[zz].reshape(tokens, width)
        part_a = dot(blk, full_a[zz].reshape(width, full_a.shape[4]))
        part_b = dot(blk, full_b[zz, :, :, :, : inner + PAD].reshape(width, inner + PAD))
        if n == 0:
            acc_a[...] = part_a
            acc_b[...] = part_b
        else:
            acc_a[...] += part_a
            acc_b[...] += part_b

    def e_rows():
        for o in range(1, WINDOW):
            copies.arrive(("h", o), "h", incoming.at[pl.ds(o * CAP, CAP)])
        by_page = [jnp.int32(0)] * per_dev
        by_conv = [jnp.int32(0)] * per_dev
        for o in range(WINDOW):
            base = ((me - o + groups) % groups) * per_dev
            seen = jnp.int32(0)
            pages = [jnp.int32(0)] * CAP
            for q in range(per_dev):
                hit = owner_dev[base + q] == me
                page = jnp.where(hit, state_page[base + q], -1)
                conv = jnp.where(hit, conv_page[base + q], -1)
                kept = accepted[base + q]
                info = (o * CAP + seen) + conv * 64 + kept * 1024
                back = page + kept * 1024
                for p in range(per_dev):
                    by_page[p] = jnp.where(page == p, info, by_page[p])
                    by_conv[p] = jnp.where(conv == p, back, by_conv[p])
                for c in range(CAP):
                    pages[c] = jnp.where(hit & (seen == c), page, pages[c])
                seen = seen + hit.astype(jnp.int32)
            for c in range(CAP):
                table[8 + o * CAP + c] = pages[c]
        for p in range(per_dev):
            table[24 + p] = jnp.minimum(by_page[p] & 63, SLOTS - 1)
            table[32 + p] = jnp.minimum((by_page[p] >> 6) & 15, per_dev - 1)
            table[40 + p] = jnp.minimum(by_page[p] >> 10, draft)
            table[48 + p] = jnp.minimum(by_conv[p] & 1023, per_dev - 1)
            table[56 + p] = jnp.minimum(by_conv[p] >> 10, draft)
        for p in range(per_dev):
            rows_full[col, p] = incoming[table[24 + p]]
        for k in range(1, mdl_size):
            copies.send(("y", k), "y", rows_full.at[col], rows_full.at[col], across[k - 1])

    def e_rows_in():
        for k in range(1, mdl_size):
            copies.arrive(("y", k), "y", rows_full.at[(col - k + mdl_size) % mdl_size])

    own_a, own_b = piece_a(0, 0), piece_b(0, 0)
    b_up(1)
    b_down(1)
    for d in range(1, XN):
        copies.send(("ax", d), "ax", own_a, own_a, xs[d - 1])
    b_side(0)
    a_up(1, 0)
    a_down(1, 0)

    owners = [owner_dev[me * per_dev + q] for q in range(per_dev)]
    slots = []
    for q in range(per_dev):
        offset = owners[q] - me
        offset = jnp.where(offset < 0, offset + groups, offset)
        rank = jnp.int32(0)
        for r in range(q):
            rank = rank + (owners[r] == owners[q]).astype(jnp.int32)
        slots.append(offset * CAP + rank)
        table[q] = jnp.minimum(slots[q], SLOTS - 1)
    load_rows.wait()
    for s in range(SLOTS):
        source = jnp.int32(0)
        for q in range(per_dev):
            source = jnp.where(slots[q] == s, q, source)
        outgoing[s] = slice_in[source]
    for o in range(1, WINDOW):
        part = pl.ds(o * CAP, CAP)
        copies.send(("h", o), "h", outgoing.at[part], incoming.at[part], ahead[o - 1])
    incoming[0:CAP] = outgoing[0:CAP]

    events = []
    for d, t in ((1, 2.0), (3, 2.1), (2, 3.0)):
        events.append((t, "ax", functools.partial(e_ax, d)))
    for s in range(1, half + 1):
        events.append((0.4 + 2.2 * s, "bz", functools.partial(e_bz, s)))
        for j, d in enumerate((0, 1, 3, 2)):
            events.append((2.6 + 5.0 * (s - 1) + 1.2 * j, "a", functools.partial(e_a, s, d)))
    for n in range(zn):
        t_bx = 3.4 + 2.2 * n
        t_a = 4.0 if n == 0 else 6.3 + 5.0 * (abs(order[n]) - 1)
        t_sib = max(t_bx + 2.5, t_a + 0.01)
        events.append((t_bx, "bx", functools.partial(e_bx, n)))
        events.append((t_bx + 2.5, "bf", functools.partial(e_bf, n)))
        events.append((t_sib + 0.02, "sib", functools.partial(e_sib, n)))
        events.append((max(t_sib + 2.0, 16.0), "proj", functools.partial(e_proj, n)))
    events.append((4.5, "rows", e_rows))
    events.append((15.9, "in", e_rows_in))
    events.sort(key=lambda e: e[0])
    for _, _, run in events:
        run()

    hist_x[...] = hist_inner[...].astype(f32)
    hist_s[...] = hist_state[...].astype(f32)
    lead = 8 - (KCONV - 1)
    series_x[:, 8:, :] = acc_b[:, :inner].astype(bf16).astype(f32).reshape(per_dev, draft, inner)
    series_s[:, 8:, :] = (
        acc_a[:, inner:].astype(bf16).astype(f32).reshape(per_dev, draft, 2 * nstate)
    )
    for p in range(per_dev):
        for j in range(KCONV - 1):
            series_x[p, lead + j : lead + j + 1, :] = hist_x[j, pl.ds(table[32 + p], 1), :]
            series_s[p, lead + j : lead + j + 1, :] = hist_s[j, pl.ds(table[32 + p], 1), :]

    def conv(series, taps):
        total = taps[0:1, :] * series[:, lead : lead + draft, :]
        for k in range(1, KCONV):
            total = total + taps[k : k + 1, :] * series[:, lead + k : lead + k + draft, :]
        return jax.nn.silu(total).reshape(tokens, total.shape[2])

    active = conv(series_x, conv_inner)
    maps = conv(series_s, conv_state)
    b_rows, c_rows = maps[:, :nstate], maps[:, nstate:]

    lane = lax.broadcasted_iota(jnp.int32, (1, PAD), 1)
    bias_row = jnp.zeros((1, PAD), f32)
    rate_row = jnp.zeros((1, PAD), f32)
    for h in range(heads):
        bias_row = jnp.where(lane == h, step_bias[h], bias_row)
        rate_row = jnp.where(lane == h, decay_log[h], rate_row)
    rate_row = jnp.exp(rate_row)
    step_raw = acc_b[:, inner:].astype(bf16).astype(f32)
    size = jax.nn.softplus(step_raw + bias_row)
    rows_i = lax.broadcasted_iota(jnp.int32, (tokens, tokens), 0)
    cols_i = lax.broadcasted_iota(jnp.int32, (tokens, tokens), 1)
    causal = (rows_i // draft == cols_i // draft) & (cols_i <= rows_i)
    decay = dot(causal.astype(f32), -size * rate_row, HIGH)
    decay_t, size_t = decay.T, size.T
    scores = dot_nt(c_rows, b_rows, HIGH)
    end_at = jnp.zeros((tokens, tokens), jnp.int32)
    for p in range(per_dev):
        end_at = jnp.where(rows_i // draft == p, p * draft + table[40 + p] - 1, end_at)
    end_decay = dot((cols_i == end_at).astype(f32), decay, HIGH)
    before = rows_i <= end_at
    chosen_w = jnp.where(before, jnp.exp(jnp.where(before, end_decay - decay, 0.0)), 0.0) * size
    grown = jnp.exp(decay)
    decay_s[...] = jnp.exp(end_decay)

    b_low = b_rows.astype(bf16)
    c_low = c_rows.astype(bf16)
    load_state.wait()
    for p in range(per_dev):
        start = state[p].reshape(inner, nstate)
        carried[p * draft : (p + 1) * draft, :] = dot_nt(
            c_low[p * draft : (p + 1) * draft, :], start.astype(bf16)
        )

    left = lax.broadcasted_iota(jnp.int32, (tokens, PAD), 1) < hdim

    def spread(values, j):
        return jnp.where(left, values[:, 2 * j : 2 * j + 1], values[:, 2 * j + 1 : 2 * j + 2])

    total = jnp.zeros((tokens, PAD), f32)
    gated_cols = []
    for j in range(heads // 2):
        cols = slice(j * PAD, (j + 1) * PAD)
        x_pair = active[:, cols]
        x_low = x_pair.astype(bf16)
        pair = []
        for h in (2 * j, 2 * j + 1):
            gap = decay[:, h : h + 1] - decay_t[h : h + 1, :]
            weight = jnp.exp(jnp.where(causal, gap, -1e30)) * scores * size_t[h : h + 1, :]
            pair.append(dot(weight.astype(bf16), x_low))
        skip = jnp.where(left, skip_gain[2 * j], skip_gain[2 * j + 1])
        y = (
            jnp.where(left, pair[0], pair[1])
            + carried[:, cols] * spread(grown, j)
            + skip * x_pair
        )
        gated = y.astype(bf16).astype(f32) * jax.nn.silu(acc_a[:, cols])
        total = total + gated * gated
        gated_cols.append((gated * norm_gain[0:1, cols]).astype(bf16))
    gated_low = jnp.concatenate(gated_cols, axis=1)
    squares[...] = dot_nt(jnp.ones((8, PAD), f32), total, HIGH)
    for k in range(1, mdl_size):
        copies.send(("s", k), "s", squares, square_parts.at[k], across[k - 1])
    far_first = sorted(range(1, mdl_size), key=lambda k: -min(k, mdl_size - k))

    def project_out(m):
        block = full_b[m, :, :, :, inner + PAD :].reshape(columns, inner)
        return dot_nt(gated_low, block)

    for k in far_first:
        m = (col + k) % mdl_size
        terms[k] = project_out(m).astype(bf16)
        copies.send(("t", k), "t", terms.at[k], parts.at[k], across[k - 1])
    own_term = project_out(col)

    picked_t = []
    for j in range(heads // 2):
        cols = slice(j * PAD, (j + 1) * PAD)
        picked_t.append((active[:, cols] * spread(chosen_w, j)).T.astype(bf16))
    picked = jnp.concatenate(picked_t, axis=0)
    row_of = lax.broadcasted_iota(jnp.int32, (tokens, nstate), 0) // draft
    stores = []
    for p in range(per_dev):
        added = dot(picked, jnp.where(row_of == p, b_low, jnp.zeros_like(b_low)))
        for h in range(heads):
            factor = decay_s[p * draft : p * draft + 1, h : h + 1]
            state[p, h] = factor * state[p, h] + added[h * hdim : (h + 1) * hdim, :]
        store = pltpu.make_async_copy(state.at[p], new_states.at[p], local_sem.at[2 + p])
        store.start()
        stores.append(store)
    for c in range(per_dev):
        for j in range(KCONV - 1):
            row = pl.ds(lead + table[56 + c] + j, 1)
            edge_x[j, c : c + 1, :] = series_x[table[48 + c], row, :]
            edge_s[j, c : c + 1, :] = series_s[table[48 + c], row, :]
    edge_inner[...] = edge_x[...].astype(bf16)
    edge_state[...] = edge_s[...].astype(bf16)

    square_parts[0] = squares[...]
    for k in range(1, mdl_size):
        copies.arrive(("s", k), "s", square_parts.at[k])
    stacked = square_parts[...].reshape(mdl_size * 8, tokens)
    eighth = jnp.full((mdl_size * 8, columns), 0.125, f32)
    mean = lax.dot_general(
        stacked, eighth, TN, preferred_element_type=f32, precision=HIGH
    ) / (mdl_size * inner)
    scale = lax.rsqrt(mean + EPSILON)
    for k in reversed(far_first):
        copies.arrive(("t", k), "t", parts.at[k])
        own_term = own_term + parts[k].astype(f32)
    result[...] = (own_term * scale).astype(bf16).reshape(per_dev, draft, columns)
    for s in range(SLOTS):
        outgoing2[s] = result[table[8 + s]]
    for o in range(1, WINDOW):
        part = pl.ds(o * CAP, CAP)
        copies.send(("r", o), "r", outgoing2.at[part], incoming2.at[part], behind[o - 1])
    incoming2[0:CAP] = outgoing2[0:CAP]

    copies.sent("a", full_a.at[pl.ds(0, half - 1)])
    copies.sent("a_last", full_a.at[0, pl.ds(0, 2)])
    copies.sent("ax", full_a.at[0, pl.ds(0, XN - 1), 0])
    copies.sent("b", full_b.at[0, pl.ds(0, half - 1)])
    copies.sent("b_last", full_b.at[0, 0, 0])
    copies.sent("bx", full_b.at[pl.ds(0, 2)])
    copies.sent("bf", full_b.at[0])
    copies.sent("sa", full_a.at[pl.ds(0, half)])
    copies.sent("sb", full_b.at[pl.ds(0, half)])
    copies.sent("h", incoming.at[pl.ds(CAP, SLOTS - CAP)])
    copies.sent("y", rows_full.at[pl.ds(1, mdl_size - 1)])
    copies.sent("s", square_parts.at[pl.ds(1, mdl_size - 1)])
    copies.sent("t", parts.at[pl.ds(1, mdl_size - 1)])
    for store in stores:
        store.wait()
    for o in range(1, WINDOW):
        copies.arrive(("r", o), "r", incoming2.at[pl.ds(o * CAP, CAP)])
    for q in range(per_dev):
        mixed[q] = incoming2[table[q]]
    copies.sent("r", incoming2.at[pl.ds(CAP, SLOTS - CAP)])


def on_device(
    hidden_in,
    z_weight,
    x_weight,
    state_proj,
    step_weight,
    step_bias,
    decay_log,
    skip_gain,
    conv_inner,
    conv_state,
    norm_gain,
    out_weight,
    state_pool,
    conv_pool_inner,
    conv_pool_state,
    owner_dev,
    state_page,
    conv_page,
    accepted,
):
    groups = lax.axis_size("req")
    mdl_size = lax.axis_size("mdl")
    per_dev, heads, hdim, nstate = state_pool.shape
    tokens, depth = hidden_in.shape
    draft = tokens // per_dev
    inner = heads * hdim
    zn = groups // (2 * XN)
    rows = z_weight.shape[0]
    width = depth // mdl_size
    columns = depth // mdl_size
    f32, bf16 = jnp.float32, jnp.bfloat16
    smem = pl.BlockSpec(memory_space=pltpu.SMEM)
    vmem = pl.BlockSpec(memory_space=pltpu.VMEM)
    hbm = pl.BlockSpec(memory_space=pl.ANY)
    hist_inner = conv_pool_inner.transpose(1, 0, 2)
    hist_state = conv_pool_state.transpose(1, 0, 2)
    edge = (KCONV - 1, per_dev)
    mixed, new_states, edge_inner, edge_state = pl.pallas_call(
        functools.partial(layer_kernel, groups, mdl_size),
        out_shape=(
            jax.ShapeDtypeStruct((per_dev, draft, columns), bf16),
            jax.ShapeDtypeStruct(state_pool.shape, state_pool.dtype),
            jax.ShapeDtypeStruct(hist_inner.shape, hist_inner.dtype),
            jax.ShapeDtypeStruct(hist_state.shape, hist_state.dtype),
        ),
        in_specs=[smem] * 7 + [vmem] * 10 + [hbm] * 2,
        out_specs=(vmem, hbm, vmem, vmem),
        scratch_shapes=[
            pltpu.VMEM((zn, XN, 2, rows, inner + 2 * nstate), bf16),
            pltpu.VMEM((zn, XN, 2, rows, 2 * inner + PAD), bf16),
            pltpu.VMEM((mdl_size, per_dev, draft, width), bf16),
            pltpu.VMEM((per_dev, draft, width), bf16),
            pltpu.VMEM((SLOTS, draft, width), bf16),
            pltpu.VMEM((SLOTS, draft, width), bf16),
            pltpu.VMEM(state_pool.shape, f32),
            pltpu.VMEM((tokens, inner + 2 * nstate), f32),
            pltpu.VMEM((tokens, inner + PAD), f32),
            pltpu.VMEM((per_dev, draft + 8, inner), f32),
            pltpu.VMEM((per_dev, draft + 8, 2 * nstate), f32),
            pltpu.VMEM(edge + (inner,), f32),
            pltpu.VMEM(edge + (2 * nstate,), f32),
            pltpu.VMEM(edge + (inner,), f32),
            pltpu.VMEM(edge + (2 * nstate,), f32),
            pltpu.VMEM((tokens, inner), f32),
            pltpu.SMEM((64,), jnp.int32),
            pltpu.VMEM((tokens, PAD), f32),
            pltpu.VMEM((mdl_size, tokens, columns), bf16),
            pltpu.VMEM((8, tokens), f32),
            pltpu.VMEM((mdl_size, tokens, columns), bf16),
            pltpu.VMEM((mdl_size, 8, tokens), f32),
            pltpu.VMEM((per_dev, draft, columns), bf16),
            pltpu.VMEM((SLOTS, draft, columns), bf16),
            pltpu.VMEM((SLOTS, draft, columns), bf16),
            pltpu.SemaphoreType.DMA((16,)),
            pltpu.SemaphoreType.DMA((120,)),
            pltpu.SemaphoreType.DMA((2 + per_dev,)),
        ],
        compiler_params=pltpu.CompilerParams(
            collective_id=0, has_side_effects=True, vmem_limit_bytes=58 << 20
        ),
        name="draft_layer",
    )(
        owner_dev,
        state_page,
        conv_page,
        accepted,
        step_bias,
        decay_log,
        skip_gain,
        z_weight,
        x_weight,
        state_proj,
        step_weight.T,
        out_weight.T,
        conv_inner,
        conv_state,
        norm_gain.reshape(1, -1),
        hist_inner,
        hist_state,
        hidden_in.reshape(per_dev, draft, depth),
        state_pool,
    )
    return (
        mixed.reshape(tokens, columns),
        new_states,
        edge_inner.transpose(1, 0, 2),
        edge_state.transpose(1, 0, 2),
    )


def solution(mesh):
    return jax.shard_map(
        on_device,
        mesh=mesh,
        in_specs=(
            P("req", None),
            P("req", "mdl"),
            P("req", "mdl"),
            P("req", None),
            P("req", "mdl"),
            P("mdl"),
            P("mdl"),
            P("mdl"),
            P(None, "mdl"),
            P(),
            P("mdl"),
            P("mdl", "req"),
            P("req", "mdl", None, None),
            P("req", None, "mdl"),
            P("req", None, None),
            P(),
            P(),
            P(),
            P(),
        ),
        out_specs=(
            P("req", "mdl"),
            P("req", "mdl", None, None),
            P("req", None, "mdl"),
            P("req", None, None),
        ),
        check_vma=False,
    )
```

```python
import functools

import jax
import jax.numpy as jnp
from jax import lax
from jax.experimental import pallas as pl
from jax.experimental.pallas import tpu as pltpu
from jax.sharding import PartitionSpec as P

KCONV = 4
CAP = 2
WINDOW = 8
SLOTS = WINDOW * CAP
XN = 4
PAD = 128
HIGH = lax.Precision.HIGHEST
EPSILON = 1e-05

ORDER = (
    ("ax", 1), ("ax", 3), ("bu", 1), ("bd", 1), ("ax", 2), ("au", 1, 0), ("ad", 1, 0), ("bl", 0),
    ("au", 1, 1), ("ad", 1, 1), ("br", 0), ("bl", 1), ("au", 1, 3), ("ad", 1, 3), ("br", 1),
    ("bl", 2), ("bu", 2), ("bd", 2), ("br", 2), ("au", 1, 2), ("ad", 1, 2), ("bf", 1),
    ("au", 2, 0), ("ad", 2, 0), ("bf", 0), ("bl", 3), ("au", 2, 1), ("ad", 2, 1), ("br", 3),
    ("au", 2, 3), ("ad", 2, 3), ("bl", 4), ("br", 4), ("bu", 3), ("bd", 3), ("bf", 3),
    ("au", 2, 2), ("ad", 2, 2), ("bf", 2), ("au", 3, 0), ("ad", 3, 0), ("bf", 4), ("bl", 5),
    ("au", 3, 1), ("ad", 3, 1), ("proj", 0), ("proj", 1), ("au", 3, 3), ("ad", 3, 3), ("br", 5),
    ("bl", 6), ("proj", 2), ("bz", 4), ("proj", 3), ("br", 6), ("bf", 5), ("au", 3, 2),
    ("ad", 3, 2), ("proj", 4), ("au", 4, 0), ("ad", 4, 3), ("proj", 5), ("br", 7), ("bl", 7),
    ("au", 4, 1), ("ad", 4, 2), ("bf", 6), ("bf", 7), ("proj", 6), ("proj", 7),
)
MESH = pl.DeviceIdType.MESH
NT = (((1,), (1,)), ((), ()))
TN = (((0,), (0,)), ((), ()))


def dot(a, b, precision=None):
    return jnp.dot(a, b, preferred_element_type=jnp.float32, precision=precision)


def dot_nt(a, b, precision=None):
    return lax.dot_general(a, b, NT, preferred_element_type=jnp.float32, precision=precision)


class Copies:
    def __init__(self, send_sem, recv_sem, anyone):
        self.send_sem, self.recv_sem, self.anyone = send_sem, recv_sem, anyone
        self.keys, self.groups = {}, {}

    def describe(self, name, group, src, dst, peer):
        k = self.keys.setdefault(name, len(self.keys))
        g = self.groups.setdefault(group, len(self.groups))
        return pltpu.make_async_remote_copy(
            src_ref=src,
            dst_ref=dst,
            send_sem=self.send_sem.at[g],
            recv_sem=self.recv_sem.at[k],
            device_id=peer,
            device_id_type=MESH,
        )

    def send(self, name, group, src, dst, peer):
        self.describe(name, group, src, dst, peer).start()

    def arrive(self, name, group, where):
        self.describe(name, group, where, where, self.anyone).wait_recv()

    def sent(self, group, whole):
        pltpu.make_async_copy(whole, whole, self.send_sem.at[self.groups[group]]).wait()


def layer_kernel(
    groups,
    mdl_size,
    owner_dev,
    state_page,
    conv_page,
    accepted,
    step_bias,
    decay_log,
    skip_gain,
    z_weight,
    x_weight,
    state_proj,
    step_t,
    out_t,
    conv_inner,
    conv_state,
    norm_gain,
    hist_inner,
    hist_state,
    hidden,
    state_pool,
    mixed,
    new_states,
    edge_inner,
    edge_state,
    full_a,
    full_b,
    rows_full,
    slice_in,
    outgoing,
    incoming,
    state,
    acc_a,
    acc_b,
    series_x,
    series_s,
    hist_x,
    hist_s,
    edge_x,
    edge_s,
    carried,
    table,
    decay_s,
    terms,
    sums,
    squares,
    parts,
    square_parts,
    result,
    outgoing2,
    incoming2,
    send_sem,
    recv_sem,
    local_sem,
):
    f32, bf16 = jnp.float32, jnp.bfloat16
    per_dev, draft, columns = mixed.shape
    tokens = per_dev * draft
    heads, hdim, nstate = state.shape[1:]
    inner = heads * hdim
    width = slice_in.shape[2]
    zn = groups // (2 * XN)
    me = lax.axis_index("req")
    col = lax.axis_index("mdl")
    core = me % 2
    x = (me // 2) % XN
    z = me // (2 * XN)

    def zi(v):
        return (v + zn) % zn

    def xi(v):
        return (v + XN) % XN

    def at(zz, xx):
        return {"req": (zi(zz) * XN + xi(xx)) * 2 + core}

    load_rows = pltpu.make_async_copy(
        hidden.at[:, :, pl.ds(pl.multiple_of(col * width, width), width)],
        slice_in,
        local_sem.at[0],
    )
    load_rows.start()
    load_state = pltpu.make_async_copy(state_pool, state, local_sem.at[1])
    load_state.start()

    sibling = {"req": me + 1 - 2 * core}
    up, down = at(z + 1, x), at(z - 1, x)
    right, left_x = at(z, x + 1), at(z, x - 1)
    xs = [at(z, x + d) for d in range(1, XN)]
    ahead = [{"req": (me + o) % groups} for o in range(1, WINDOW)]
    behind = [{"req": (me - o + groups) % groups} for o in range(1, WINDOW)]
    across = [{"mdl": (col + k) % mdl_size} for k in range(1, mdl_size)]
    peers = [sibling, up, down] + xs + ahead + behind + across
    barrier = pltpu.get_barrier_semaphore()
    for peer in peers:
        pl.semaphore_signal(barrier, inc=1, device_id=peer, device_id_type=MESH)

    full_a[z, x, core, :, :inner] = z_weight[...]
    full_a[z, x, core, :, inner:] = state_proj[...]
    full_b[z, x, core, :, :inner] = x_weight[...]
    place = (
        lax.broadcasted_iota(jnp.int32, (heads, PAD), 0)
        == lax.broadcasted_iota(jnp.int32, (heads, PAD), 1)
    ).astype(f32)
    full_b[z, x, core, :, inner : inner + PAD] = lax.dot_general(
        step_t[...].astype(f32), place, TN, preferred_element_type=f32, precision=HIGH
    ).astype(bf16)
    full_b[z, x, core, :, inner + PAD :] = out_t[...]
    owners = [owner_dev[me * per_dev + q] for q in range(per_dev)]
    slots = []
    for q in range(per_dev):
        offset = owners[q] - me
        offset = jnp.where(offset < 0, offset + groups, offset)
        rank = jnp.int32(0)
        for r in range(q):
            rank = rank + (owners[r] == owners[q]).astype(jnp.int32)
        slots.append(offset * CAP + rank)
        table[q] = jnp.minimum(slots[q], SLOTS - 1)
    load_rows.wait()
    for s in range(SLOTS):
        source = jnp.int32(0)
        for q in range(per_dev):
            source = jnp.where(slots[q] == s, q, source)
        outgoing[s] = slice_in[source]
    pl.semaphore_wait(barrier, len(peers))

    copies = Copies(send_sem, recv_sem, up)
    half = zn // 2
    rows = full_a.shape[3]
    halves = (pl.ds(0, rows // 2), pl.ds(rows // 2, rows // 2))
    order = [0]
    for s in range(1, half):
        order += [-s, s]
    order.append(-half)
    place_of = {d: n for n, d in enumerate(order)}

    def piece_a(dz, dx):
        return full_a.at[zi(z + dz), xi(x + dx), core]

    def piece_b(dz, dx):
        return full_b.at[zi(z + dz), xi(x + dx), core]

    def share_a(dz, dx):
        p = piece_a(dz, dx)
        copies.send(("sa", place_of[dz]), "sa", p, p, sibling)

    def share_b(dz, dx):
        p = piece_b(dz, dx)
        copies.send(("sb", place_of[dz]), "sb", p, p, sibling)

    def a_up(s, d):
        group = "a_last" if s == half else "a"
        copies.send(("au", s, d), group, piece_a(1 - s, -d), piece_a(1 - s, -d), up)

    def a_down(s, d):
        group = "a_last" if s == half else "a"
        copies.send(("ad", s, d), group, piece_a(s - 1, -d), piece_a(s - 1, -d), down)

    up_last, down_last = range(0, XN // 2), range(XN // 2, XN)

    def b_up(s):
        p = piece_b(1 - s, 0)
        if s == half:
            copies.send(("bu", s), "b_last", p.at[halves[0]], p.at[halves[0]], up)
        else:
            copies.send(("bu", s), "b", p, p, up)

    def b_down(s):
        p = piece_b(s - 1, 0)
        if s == half:
            copies.send(("bd", s), "b_last", p.at[halves[1]], p.at[halves[1]], down)
        else:
            copies.send(("bd", s), "b", p, p, down)

    def b_side(n):
        p = piece_b(order[n], 0)
        copies.send(("br", n), "bx", p, p, right)
        copies.send(("bl", n), "bx", p, p, left_x)

    def e_ax(d):
        copies.arrive(("ax", d), "ax", piece_a(0, -d))
        a_up(1, d)
        a_down(1, d)
        share_a(0, -d)

    def e_bu(s):
        copies.arrive(("bu", s), "b", piece_b(-s, 0))
        b_up(s + 1)
        b_side(place_of[-s])
        share_b(-s, 0)

    def e_bd(s):
        copies.arrive(("bd", s), "b", piece_b(s, 0))
        b_down(s + 1)
        b_side(place_of[s])
        share_b(s, 0)

    def e_bz(s):
        copies.arrive(("bu", s), "b_last", piece_b(-s, 0).at[halves[0]])
        copies.arrive(("bd", s), "b_last", piece_b(-s, 0).at[halves[1]])
        b_side(place_of[-s])
        share_b(-s, 0)

    def e_au(s, d):
        copies.arrive(("au", s, d), "a" if s < half else "a_last", piece_a(-s, -d))
        if s + 1 < half or (s < half and d in up_last):
            a_up(s + 1, d)
        share_a(-s, -d)

    def e_ad(s, d):
        copies.arrive(("ad", s, d), "a" if s < half else "a_last", piece_a(s, -d))
        if s + 1 < half or (s < half and d in down_last):
            a_down(s + 1, d)
        share_a(s if s < half else -s, -d)

    def e_br(n):
        p = piece_b(order[n], -1)
        copies.arrive(("br", n), "bx", p)
        if n % 2 == 0:
            copies.send(("bf", n), "bf", p, p, right)
        share_b(order[n], -1)

    def e_bl(n):
        p = piece_b(order[n], 1)
        copies.arrive(("bl", n), "bx", p)
        if n % 2 == 1:
            copies.send(("bf", n), "bf", p, p, left_x)
        share_b(order[n], 1)

    def e_bf(n):
        copies.arrive(("bf", n), "bf", piece_b(order[n], 2))
        share_b(order[n], 2)

    def e_proj(n):
        zz = zi(z + order[n])
        copies.arrive(("sa", n), "sa", full_a.at[zz, :, 1 - core])
        copies.arrive(("sb", n), "sb", full_b.at[zz, :, 1 - core])
        blk = rows_full[zz].reshape(tokens, width)
        part_a = dot(blk, full_a[zz].reshape(width, full_a.shape[4]))
        part_b = dot(blk, full_b[zz, :, :, :, : inner + PAD].reshape(width, inner + PAD))
        if n == 0:
            acc_a[...] = part_a
            acc_b[...] = part_b
        else:
            acc_a[...] += part_a
            acc_b[...] += part_b

    def e_table(o):
        base = ((me - o + groups) % groups) * per_dev
        seen = jnp.int32(0)
        pages = [jnp.int32(0)] * CAP
        for q in range(per_dev):
            hit = owner_dev[base + q] == me
            page = jnp.where(hit, state_page[base + q], -1)
            conv = jnp.where(hit, conv_page[base + q], -1)
            kept = accepted[base + q]
            info = (o * CAP + seen) + conv * 64 + kept * 1024
            back = page + kept * 1024
            for p in range(per_dev):
                by_page[p] = jnp.where(page == p, info, by_page[p])
                by_conv[p] = jnp.where(conv == p, back, by_conv[p])
            for c in range(CAP):
                pages[c] = jnp.where(hit & (seen == c), page, pages[c])
            seen = seen + hit.astype(jnp.int32)
        for c in range(CAP):
            table[8 + o * CAP + c] = pages[c]

    by_page = [jnp.int32(0)] * per_dev
    by_conv = [jnp.int32(0)] * per_dev

    def e_rows():
        for o in range(1, WINDOW):
            copies.arrive(("h", o), "h", incoming.at[pl.ds(o * CAP, CAP)])
        for p in range(per_dev):
            table[24 + p] = jnp.minimum(by_page[p] & 63, SLOTS - 1)
            table[32 + p] = jnp.minimum((by_page[p] >> 6) & 15, per_dev - 1)
            table[40 + p] = jnp.minimum(by_page[p] >> 10, draft)
            table[48 + p] = jnp.minimum(by_conv[p] & 1023, per_dev - 1)
            table[56 + p] = jnp.minimum(by_conv[p] >> 10, draft)
        for p in range(per_dev):
            rows_full[col, p] = incoming[table[24 + p]]
        for k in range(1, mdl_size):
            copies.send(("y", k), "y", rows_full.at[col], rows_full.at[col], across[k - 1])

    def e_rows_in():
        for k in range(1, mdl_size):
            copies.arrive(("y", k), "y", rows_full.at[(col - k + mdl_size) % mdl_size])

    for o in range(1, WINDOW):
        part = pl.ds(o * CAP, CAP)
        copies.send(("h", o), "h", outgoing.at[part], incoming.at[part], ahead[o - 1])
    incoming[0:CAP] = outgoing[0:CAP]

    own_a, own_b = piece_a(0, 0), piece_b(0, 0)
    b_up(1)
    b_down(1)
    for d in range(1, XN):
        copies.send(("ax", d), "ax", own_a, own_a, xs[d - 1])
    a_up(1, 0)
    a_down(1, 0)
    b_side(0)
    share_a(0, 0)
    share_b(0, 0)


    run = {
        "ax": e_ax,
        "bu": e_bu,
        "bd": e_bd,
        "bz": e_bz,
        "au": e_au,
        "ad": e_ad,
        "br": e_br,
        "bl": e_bl,
        "bf": e_bf,
        "proj": e_proj,
    }
    for o in range(WINDOW):
        e_table(o)
    started, projected = False, False
    for event in ORDER:
        if event[0] == "au" and not started:
            started = True
            e_rows()
        if event[0] == "proj" and not projected:
            projected = True
            e_rows_in()
        run[event[0]](*event[1:])

    hist_x[...] = hist_inner[...].astype(f32)
    hist_s[...] = hist_state[...].astype(f32)
    lead = 8 - (KCONV - 1)
    series_x[:, 8:, :] = acc_b[:, :inner].astype(bf16).astype(f32).reshape(per_dev, draft, inner)
    series_s[:, 8:, :] = (
        acc_a[:, inner:].astype(bf16).astype(f32).reshape(per_dev, draft, 2 * nstate)
    )
    for p in range(per_dev):
        for j in range(KCONV - 1):
            series_x[p, lead + j : lead + j + 1, :] = hist_x[j, pl.ds(table[32 + p], 1), :]
            series_s[p, lead + j : lead + j + 1, :] = hist_s[j, pl.ds(table[32 + p], 1), :]

    def conv(series, taps):
        total = taps[0:1, :] * series[:, lead : lead + draft, :]
        for k in range(1, KCONV):
            total = total + taps[k : k + 1, :] * series[:, lead + k : lead + k + draft, :]
        return jax.nn.silu(total).reshape(tokens, total.shape[2])

    active = conv(series_x, conv_inner)
    maps = conv(series_s, conv_state)
    b_rows, c_rows = maps[:, :nstate], maps[:, nstate:]

    lane = lax.broadcasted_iota(jnp.int32, (1, PAD), 1)
    bias_row = jnp.zeros((1, PAD), f32)
    rate_row = jnp.zeros((1, PAD), f32)
    for h in range(heads):
        bias_row = jnp.where(lane == h, step_bias[h], bias_row)
        rate_row = jnp.where(lane == h, decay_log[h], rate_row)
    rate_row = jnp.exp(rate_row)
    step_raw = acc_b[:, inner:].astype(bf16).astype(f32)
    size = jax.nn.softplus(step_raw + bias_row)
    rows_i = lax.broadcasted_iota(jnp.int32, (tokens, tokens), 0)
    cols_i = lax.broadcasted_iota(jnp.int32, (tokens, tokens), 1)
    causal = (rows_i // draft == cols_i // draft) & (cols_i <= rows_i)
    decay = dot(causal.astype(f32), -size * rate_row, HIGH)
    decay_t, size_t = decay.T, size.T
    scores = dot_nt(c_rows, b_rows, HIGH)
    end_at = jnp.zeros((tokens, tokens), jnp.int32)
    for p in range(per_dev):
        end_at = jnp.where(rows_i // draft == p, p * draft + table[40 + p] - 1, end_at)
    end_decay = dot((cols_i == end_at).astype(f32), decay, HIGH)
    before = rows_i <= end_at
    chosen_w = jnp.where(before, jnp.exp(jnp.where(before, end_decay - decay, 0.0)), 0.0) * size
    grown = jnp.exp(decay)
    decay_s[...] = jnp.exp(end_decay)

    b_low = b_rows.astype(bf16)
    c_low = c_rows.astype(bf16)
    c_rest = (c_rows - c_low.astype(f32)).astype(bf16)
    load_state.wait()
    for p in range(per_dev):
        start = state[p].reshape(inner, nstate)
        mine = slice(p * draft, (p + 1) * draft)
        both = jnp.concatenate([c_low[mine], c_rest[mine]], axis=0)
        found = dot_nt(both, start.astype(bf16))
        carried[mine, :] = found[:draft] + found[draft:]

    left = lax.broadcasted_iota(jnp.int32, (tokens, PAD), 1) < hdim

    def spread(values, j):
        return jnp.where(left, values[:, 2 * j : 2 * j + 1], values[:, 2 * j + 1 : 2 * j + 2])

    total = jnp.zeros((tokens, PAD), f32)
    gated_cols = []
    for j in range(heads // 2):
        cols = slice(j * PAD, (j + 1) * PAD)
        x_pair = active[:, cols]
        x_low = x_pair.astype(bf16)
        x_rest = (x_pair - x_low.astype(f32)).astype(bf16)
        pair = []
        for h in (2 * j, 2 * j + 1):
            gap = decay[:, h : h + 1] - decay_t[h : h + 1, :]
            weight = jnp.exp(jnp.where(causal, gap, -1e30)) * scores * size_t[h : h + 1, :]
            w_low = weight.astype(bf16)
            w_rest = (weight - w_low.astype(f32)).astype(bf16)
            pair.append(dot(w_low, x_low) + dot(w_rest, x_low) + dot(w_low, x_rest))
        skip = jnp.where(left, skip_gain[2 * j], skip_gain[2 * j + 1])
        y = (
            jnp.where(left, pair[0], pair[1])
            + carried[:, cols] * spread(grown, j)
            + skip * x_pair
        )
        gated = y.astype(bf16).astype(f32) * jax.nn.silu(acc_a[:, cols])
        total = total + gated * gated
        gated_cols.append((gated * norm_gain[0:1, cols]).astype(bf16))
    gated_low = jnp.concatenate(gated_cols, axis=1)
    squares[...] = dot_nt(jnp.ones((8, PAD), f32), total, HIGH)
    for k in range(1, mdl_size):
        copies.send(("s", k), "s", squares, square_parts.at[k], across[k - 1])

    def project_out(k):
        m = (col + k + mdl_size) % mdl_size
        block = full_b[m, :, :, :, inner + PAD :].reshape(columns, inner)
        return dot_nt(gated_low, block)

    def ring(k):
        return across[k % mdl_size - 1]

    low, high = pl.ds(0, tokens // 2), pl.ds(tokens // 2, tokens // 2)
    terms[4] = project_out(4).astype(bf16)
    copies.send(("t4u",), "t", terms.at[4, low], parts.at[2, low], ring(2))
    copies.send(("t4d",), "t", terms.at[4, high], parts.at[2, high], ring(-2))
    for k, name, slot in ((3, "t3u", 0), (-3, "t3d", 1), (1, "t1u", 3), (-1, "t1d", 4)):
        terms[k % mdl_size] = project_out(k).astype(bf16)
        towards = 1 if k > 0 else -1
        copies.send((name,), "t", terms.at[k % mdl_size], parts.at[slot], ring(towards))
    sums[0] = project_out(2)
    sums[1] = project_out(-2)
    own_term = project_out(0)

    picked_t = []
    for j in range(heads // 2):
        cols = slice(j * PAD, (j + 1) * PAD)
        picked_t.append((active[:, cols] * spread(chosen_w, j)).T.astype(bf16))
    picked = jnp.concatenate(picked_t, axis=0)
    row_of = lax.broadcasted_iota(jnp.int32, (tokens, nstate), 0) // draft
    stores = []
    for p in range(per_dev):
        added = dot(picked, jnp.where(row_of == p, b_low, jnp.zeros_like(b_low)))
        for h in range(heads):
            factor = decay_s[p * draft : p * draft + 1, h : h + 1]
            state[p, h] = factor * state[p, h] + added[h * hdim : (h + 1) * hdim, :]
        store = pltpu.make_async_copy(state.at[p], new_states.at[p], local_sem.at[2 + p])
        store.start()
        stores.append(store)
    copies.arrive(("t3u",), "t", parts.at[0])
    copies.arrive(("t4u",), "t", parts.at[2, low])
    sums[0] += parts[0].astype(f32)
    sums[0, low, :] += parts[2, low, :].astype(f32)
    terms[2] = sums[0].astype(bf16)
    copies.send(("t2u",), "t", terms.at[2], parts.at[5], ring(2))
    copies.arrive(("t3d",), "t", parts.at[1])
    copies.arrive(("t4d",), "t", parts.at[2, high])
    sums[1] += parts[1].astype(f32)
    sums[1, high, :] += parts[2, high, :].astype(f32)
    terms[mdl_size - 2] = sums[1].astype(bf16)
    copies.send(("t2d",), "t", terms.at[mdl_size - 2], parts.at[6], ring(-2))
    for c in range(per_dev):
        for j in range(KCONV - 1):
            row = pl.ds(lead + table[56 + c] + j, 1)
            edge_x[j, c : c + 1, :] = series_x[table[48 + c], row, :]
            edge_s[j, c : c + 1, :] = series_s[table[48 + c], row, :]
    edge_inner[...] = edge_x[...].astype(bf16)
    edge_state[...] = edge_s[...].astype(bf16)

    square_parts[0] = squares[...]
    for k in range(1, mdl_size):
        copies.arrive(("s", k), "s", square_parts.at[k])
    stacked = square_parts[...].reshape(mdl_size * 8, tokens)
    eighth = jnp.full((mdl_size * 8, columns), 0.125, f32)
    mean = lax.dot_general(
        stacked, eighth, TN, preferred_element_type=f32, precision=HIGH
    ) / (mdl_size * inner)
    scale = lax.rsqrt(mean + EPSILON)
    for name, slot in (("t1u", 3), ("t1d", 4), ("t2u", 5), ("t2d", 6)):
        copies.arrive((name,), "t", parts.at[slot])
        own_term = own_term + parts[slot].astype(f32)
    result[...] = (own_term * scale).astype(bf16).reshape(per_dev, draft, columns)
    for s in range(SLOTS):
        outgoing2[s] = result[table[8 + s]]
    for o in range(1, WINDOW):
        part = pl.ds(o * CAP, CAP)
        copies.send(("r", o), "r", outgoing2.at[part], incoming2.at[part], behind[o - 1])
    incoming2[0:CAP] = outgoing2[0:CAP]

    copies.sent("a", full_a.at[pl.ds(0, half - 1)])
    copies.sent("a_last", full_a.at[0, pl.ds(0, 2)])
    copies.sent("ax", full_a.at[0, pl.ds(0, XN - 1), 0])
    copies.sent("b", full_b.at[0, pl.ds(0, half - 1)])
    copies.sent("b_last", full_b.at[0, 0, 0])
    copies.sent("bx", full_b.at[pl.ds(0, 2)])
    copies.sent("bf", full_b.at[0])
    copies.sent("sa", full_a.at[pl.ds(0, half)])
    copies.sent("sb", full_b.at[pl.ds(0, half)])
    copies.sent("h", incoming.at[pl.ds(CAP, SLOTS - CAP)])
    copies.sent("y", rows_full.at[pl.ds(1, mdl_size - 1)])
    copies.sent("s", square_parts.at[pl.ds(1, mdl_size - 1)])
    copies.sent("t", parts.at[pl.ds(1, mdl_size - 1)])
    for store in stores:
        store.wait()
    for o in range(1, WINDOW):
        copies.arrive(("r", o), "r", incoming2.at[pl.ds(o * CAP, CAP)])
    for q in range(per_dev):
        mixed[q] = incoming2[table[q]]
    copies.sent("r", incoming2.at[pl.ds(CAP, SLOTS - CAP)])


def store_kernel(mixed, states, edge_inner, edge_state, *outs):
    for source, out in zip((mixed, states, edge_inner, edge_state), outs, strict=True):
        out[...] = source[...]


def store(mixed, states, edge_inner, edge_state):
    steps = 4
    chunk = (states.shape[0] // steps,) + states.shape[1:]
    state_spec = pl.BlockSpec(chunk, lambda k: (k, 0, 0, 0))

    def whole(a):
        return pl.BlockSpec(a.shape, lambda k: (0,) * len(a.shape))

    specs = (whole(mixed), state_spec, whole(edge_inner), whole(edge_state))
    arrays = (mixed, states, edge_inner, edge_state)
    return pl.pallas_call(
        store_kernel,
        grid=(steps,),
        out_shape=tuple(jax.ShapeDtypeStruct(a.shape, a.dtype) for a in arrays),
        in_specs=list(specs),
        out_specs=specs,
        compiler_params=pltpu.CompilerParams(vmem_limit_bytes=60 << 20),
        name="store_results",
    )(*arrays)


def on_device(
    hidden_in,
    z_weight,
    x_weight,
    state_proj,
    step_weight,
    step_bias,
    decay_log,
    skip_gain,
    conv_inner,
    conv_state,
    norm_gain,
    out_weight,
    state_pool,
    conv_pool_inner,
    conv_pool_state,
    owner_dev,
    state_page,
    conv_page,
    accepted,
):
    groups = lax.axis_size("req")
    mdl_size = lax.axis_size("mdl")
    per_dev, heads, hdim, nstate = state_pool.shape
    tokens, depth = hidden_in.shape
    draft = tokens // per_dev
    inner = heads * hdim
    zn = groups // (2 * XN)
    rows = z_weight.shape[0]
    width = depth // mdl_size
    columns = depth // mdl_size
    f32, bf16 = jnp.float32, jnp.bfloat16
    smem = pl.BlockSpec(memory_space=pltpu.SMEM)
    vmem = pl.BlockSpec(memory_space=pltpu.VMEM)
    hbm = pl.BlockSpec(memory_space=pl.ANY)
    hist_inner = conv_pool_inner.transpose(1, 0, 2)
    hist_state = conv_pool_state.transpose(1, 0, 2)
    edge = (KCONV - 1, per_dev)
    mixed, new_states, edge_inner, edge_state = pl.pallas_call(
        functools.partial(layer_kernel, groups, mdl_size),
        out_shape=(
            jax.ShapeDtypeStruct((per_dev, draft, columns), bf16),
            jax.ShapeDtypeStruct(state_pool.shape, state_pool.dtype),
            jax.ShapeDtypeStruct(hist_inner.shape, hist_inner.dtype),
            jax.ShapeDtypeStruct(hist_state.shape, hist_state.dtype),
        ),
        in_specs=[smem] * 7 + [vmem] * 10 + [hbm] * 2,
        out_specs=(vmem, hbm, vmem, vmem),
        scratch_shapes=[
            pltpu.VMEM((zn, XN, 2, rows, inner + 2 * nstate), bf16),
            pltpu.VMEM((zn, XN, 2, rows, 2 * inner + PAD), bf16),
            pltpu.VMEM((mdl_size, per_dev, draft, width), bf16),
            pltpu.VMEM((per_dev, draft, width), bf16),
            pltpu.VMEM((SLOTS, draft, width), bf16),
            pltpu.VMEM((SLOTS, draft, width), bf16),
            pltpu.VMEM(state_pool.shape, f32),
            pltpu.VMEM((tokens, inner + 2 * nstate), f32),
            pltpu.VMEM((tokens, inner + PAD), f32),
            pltpu.VMEM((per_dev, draft + 8, inner), f32),
            pltpu.VMEM((per_dev, draft + 8, 2 * nstate), f32),
            pltpu.VMEM(edge + (inner,), f32),
            pltpu.VMEM(edge + (2 * nstate,), f32),
            pltpu.VMEM(edge + (inner,), f32),
            pltpu.VMEM(edge + (2 * nstate,), f32),
            pltpu.VMEM((tokens, inner), f32),
            pltpu.SMEM((64,), jnp.int32),
            pltpu.VMEM((tokens, PAD), f32),
            pltpu.VMEM((mdl_size, tokens, columns), bf16),
            pltpu.VMEM((2, tokens, columns), f32),
            pltpu.VMEM((8, tokens), f32),
            pltpu.VMEM((mdl_size, tokens, columns), bf16),
            pltpu.VMEM((mdl_size, 8, tokens), f32),
            pltpu.VMEM((per_dev, draft, columns), bf16),
            pltpu.VMEM((SLOTS, draft, columns), bf16),
            pltpu.VMEM((SLOTS, draft, columns), bf16),
            pltpu.SemaphoreType.DMA((16,)),
            pltpu.SemaphoreType.DMA((120,)),
            pltpu.SemaphoreType.DMA((2 + per_dev,)),
        ],
        compiler_params=pltpu.CompilerParams(
            collective_id=0, has_side_effects=True, vmem_limit_bytes=58 << 20
        ),
        name="draft_layer",
    )(
        owner_dev,
        state_page,
        conv_page,
        accepted,
        step_bias,
        decay_log,
        skip_gain,
        z_weight,
        x_weight,
        state_proj,
        step_weight.T,
        out_weight.T,
        conv_inner,
        conv_state,
        norm_gain.reshape(1, -1),
        hist_inner,
        hist_state,
        hidden_in.reshape(per_dev, draft, depth),
        state_pool,
    )
    mixed, new_states, edge_inner, edge_state = store(
        mixed, new_states, edge_inner, edge_state
    )
    return (
        mixed.reshape(tokens, columns),
        new_states,
        edge_inner.transpose(1, 0, 2),
        edge_state.transpose(1, 0, 2),
    )


def solution(mesh):
    return jax.shard_map(
        on_device,
        mesh=mesh,
        in_specs=(
            P("req", None),
            P("req", "mdl"),
            P("req", "mdl"),
            P("req", None),
            P("req", "mdl"),
            P("mdl"),
            P("mdl"),
            P("mdl"),
            P(None, "mdl"),
            P(),
            P("mdl"),
            P("mdl", "req"),
            P("req", "mdl", None, None),
            P("req", None, "mdl"),
            P("req", None, None),
            P(),
            P(),
            P(),
            P(),
        ),
        out_specs=(
            P("req", "mdl"),
            P("req", "mdl", None, None),
            P("req", None, "mdl"),
            P("req", None, None),
        ),
        check_vma=False,
    )
```

```python
import functools

import jax
import jax.numpy as jnp
from jax import lax
from jax.experimental import pallas as pl
from jax.experimental.pallas import tpu as pltpu
from jax.sharding import PartitionSpec as P

KCONV = 4
CAP = 2
WINDOW = 8
SLOTS = WINDOW * CAP
XN = 4
PAD = 128
HIGH = lax.Precision.HIGHEST
EPSILON = 1e-05

ORDER = (
    ("ax", 1), ("ax", 3), ("bu", 1), ("bd", 1), ("ax", 2), ("au", 1, 0), ("ad", 1, 0), ("bl", 0),
    ("au", 1, 1), ("ad", 1, 1), ("br", 0), ("bl", 1), ("au", 1, 3), ("ad", 1, 3), ("br", 1),
    ("bl", 2), ("bu", 2), ("bd", 2), ("br", 2), ("au", 1, 2), ("ad", 1, 2), ("bf", 1),
    ("au", 2, 0), ("ad", 2, 0), ("bf", 0), ("bl", 3), ("au", 2, 1), ("ad", 2, 1), ("br", 3),
    ("au", 2, 3), ("ad", 2, 3), ("bl", 4), ("br", 4), ("bu", 3), ("bd", 3), ("bf", 3),
    ("au", 2, 2), ("ad", 2, 2), ("bf", 2), ("au", 3, 0), ("ad", 3, 0), ("bf", 4), ("bl", 5),
    ("au", 3, 1), ("ad", 3, 1), ("proj", 0), ("proj", 1), ("au", 3, 3), ("ad", 3, 3), ("br", 5),
    ("bl", 6), ("proj", 2), ("bz", 4), ("proj", 3), ("br", 6), ("bf", 5), ("au", 3, 2),
    ("ad", 3, 2), ("proj", 4), ("au", 4, 0), ("ad", 4, 3), ("proj", 5), ("br", 7), ("bl", 7),
    ("au", 4, 1), ("ad", 4, 2), ("bf", 6), ("bf", 7), ("proj", 6), ("proj", 7),
)
MESH = pl.DeviceIdType.MESH
NT = (((1,), (1,)), ((), ()))
TN = (((0,), (0,)), ((), ()))


def dot(a, b, precision=None):
    return jnp.dot(a, b, preferred_element_type=jnp.float32, precision=precision)


def dot_nt(a, b, precision=None):
    return lax.dot_general(a, b, NT, preferred_element_type=jnp.float32, precision=precision)


class Copies:
    def __init__(self, send_sem, recv_sem, anyone):
        self.send_sem, self.recv_sem, self.anyone = send_sem, recv_sem, anyone
        self.keys, self.groups = {}, {}

    def describe(self, name, group, src, dst, peer):
        k = self.keys.setdefault(name, len(self.keys))
        g = self.groups.setdefault(group, len(self.groups))
        return pltpu.make_async_remote_copy(
            src_ref=src,
            dst_ref=dst,
            send_sem=self.send_sem.at[g],
            recv_sem=self.recv_sem.at[k],
            device_id=peer,
            device_id_type=MESH,
        )

    def send(self, name, group, src, dst, peer):
        self.describe(name, group, src, dst, peer).start()

    def arrive(self, name, group, where):
        self.describe(name, group, where, where, self.anyone).wait_recv()

    def sent(self, group, whole):
        pltpu.make_async_copy(whole, whole, self.send_sem.at[self.groups[group]]).wait()


def layer_kernel(
    groups,
    mdl_size,
    owner_dev,
    state_page,
    conv_page,
    accepted,
    step_bias,
    decay_log,
    skip_gain,
    z_weight,
    x_weight,
    state_proj,
    step_t,
    out_t,
    conv_inner,
    conv_state,
    norm_gain,
    hist_inner,
    hist_state,
    hidden,
    state_pool,
    mixed,
    new_states,
    edge_inner,
    edge_state,
    full_a,
    full_b,
    rows_full,
    slice_in,
    outgoing,
    incoming,
    state,
    state_low,
    acc_a,
    acc_b,
    series_x,
    series_s,
    hist_x,
    hist_s,
    edge_x,
    edge_s,
    carried,
    table,
    decay_s,
    terms,
    sums,
    squares,
    parts,
    square_parts,
    result,
    outgoing2,
    incoming2,
    send_sem,
    recv_sem,
    local_sem,
):
    f32, bf16 = jnp.float32, jnp.bfloat16
    per_dev, draft, columns = mixed.shape
    tokens = per_dev * draft
    heads, hdim, nstate = state.shape[1:]
    inner = heads * hdim
    width = slice_in.shape[2]
    zn = groups // (2 * XN)
    me = lax.axis_index("req")
    col = lax.axis_index("mdl")
    core = me % 2
    x = (me // 2) % XN
    z = me // (2 * XN)

    def zi(v):
        return (v + zn) % zn

    def xi(v):
        return (v + XN) % XN

    def at(zz, xx):
        return {"req": (zi(zz) * XN + xi(xx)) * 2 + core}

    load_rows = pltpu.make_async_copy(
        hidden.at[:, :, pl.ds(pl.multiple_of(col * width, width), width)],
        slice_in,
        local_sem.at[0],
    )
    load_rows.start()
    load_state = pltpu.make_async_copy(state_pool, state, local_sem.at[1])
    load_state.start()

    sibling = {"req": me + 1 - 2 * core}
    up, down = at(z + 1, x), at(z - 1, x)
    right, left_x = at(z, x + 1), at(z, x - 1)
    xs = [at(z, x + d) for d in range(1, XN)]
    ahead = [{"req": (me + o) % groups} for o in range(1, WINDOW)]
    behind = [{"req": (me - o + groups) % groups} for o in range(1, WINDOW)]
    across = [{"mdl": (col + k) % mdl_size} for k in range(1, mdl_size)]
    peers = [sibling, up, down] + xs + ahead + behind + across
    barrier = pltpu.get_barrier_semaphore()
    for peer in peers:
        pl.semaphore_signal(barrier, inc=1, device_id=peer, device_id_type=MESH)

    full_a[z, x, core, :, :inner] = z_weight[...]
    full_a[z, x, core, :, inner:] = state_proj[...]
    full_b[z, x, core, :, :inner] = x_weight[...]
    place = (
        lax.broadcasted_iota(jnp.int32, (heads, PAD), 0)
        == lax.broadcasted_iota(jnp.int32, (heads, PAD), 1)
    ).astype(f32)
    full_b[z, x, core, :, inner : inner + PAD] = lax.dot_general(
        step_t[...].astype(f32), place, TN, preferred_element_type=f32, precision=HIGH
    ).astype(bf16)
    full_b[z, x, core, :, inner + PAD :] = out_t[...]
    owners = [owner_dev[me * per_dev + q] for q in range(per_dev)]
    slots = []
    for q in range(per_dev):
        offset = owners[q] - me
        offset = jnp.where(offset < 0, offset + groups, offset)
        rank = jnp.int32(0)
        for r in range(q):
            rank = rank + (owners[r] == owners[q]).astype(jnp.int32)
        slots.append(offset * CAP + rank)
        table[q] = jnp.minimum(slots[q], SLOTS - 1)
    load_rows.wait()
    for s in range(SLOTS):
        source = jnp.int32(0)
        for q in range(per_dev):
            source = jnp.where(slots[q] == s, q, source)
        outgoing[s] = slice_in[source]
    pl.semaphore_wait(barrier, len(peers))

    copies = Copies(send_sem, recv_sem, up)
    half = zn // 2
    rows = full_a.shape[3]
    halves = (pl.ds(0, rows // 2), pl.ds(rows // 2, rows // 2))
    order = [0]
    for s in range(1, half):
        order += [-s, s]
    order.append(-half)
    place_of = {d: n for n, d in enumerate(order)}

    def piece_a(dz, dx):
        return full_a.at[zi(z + dz), xi(x + dx), core]

    def piece_b(dz, dx):
        return full_b.at[zi(z + dz), xi(x + dx), core]

    def share_a(dz, dx):
        p = piece_a(dz, dx)
        copies.send(("sa", place_of[dz]), "sa", p, p, sibling)

    def share_b(dz, dx):
        p = piece_b(dz, dx)
        copies.send(("sb", place_of[dz]), "sb", p, p, sibling)

    def a_up(s, d):
        group = "a_last" if s == half else "a"
        copies.send(("au", s, d), group, piece_a(1 - s, -d), piece_a(1 - s, -d), up)

    def a_down(s, d):
        group = "a_last" if s == half else "a"
        copies.send(("ad", s, d), group, piece_a(s - 1, -d), piece_a(s - 1, -d), down)

    up_last, down_last = range(0, XN // 2), range(XN // 2, XN)

    def b_up(s):
        p = piece_b(1 - s, 0)
        if s == half:
            copies.send(("bu", s), "b_last", p.at[halves[0]], p.at[halves[0]], up)
        else:
            copies.send(("bu", s), "b", p, p, up)

    def b_down(s):
        p = piece_b(s - 1, 0)
        if s == half:
            copies.send(("bd", s), "b_last", p.at[halves[1]], p.at[halves[1]], down)
        else:
            copies.send(("bd", s), "b", p, p, down)

    def b_side(n):
        p = piece_b(order[n], 0)
        copies.send(("br", n), "bx", p, p, right)
        copies.send(("bl", n), "bx", p, p, left_x)

    def e_ax(d):
        copies.arrive(("ax", d), "ax", piece_a(0, -d))
        a_up(1, d)
        a_down(1, d)
        share_a(0, -d)

    def e_bu(s):
        copies.arrive(("bu", s), "b", piece_b(-s, 0))
        b_up(s + 1)
        b_side(place_of[-s])
        share_b(-s, 0)

    def e_bd(s):
        copies.arrive(("bd", s), "b", piece_b(s, 0))
        b_down(s + 1)
        b_side(place_of[s])
        share_b(s, 0)

    def e_bz(s):
        copies.arrive(("bu", s), "b_last", piece_b(-s, 0).at[halves[0]])
        copies.arrive(("bd", s), "b_last", piece_b(-s, 0).at[halves[1]])
        b_side(place_of[-s])
        share_b(-s, 0)

    def e_au(s, d):
        copies.arrive(("au", s, d), "a" if s < half else "a_last", piece_a(-s, -d))
        if s + 1 < half or (s < half and d in up_last):
            a_up(s + 1, d)
        share_a(-s, -d)

    def e_ad(s, d):
        copies.arrive(("ad", s, d), "a" if s < half else "a_last", piece_a(s, -d))
        if s + 1 < half or (s < half and d in down_last):
            a_down(s + 1, d)
        share_a(s if s < half else -s, -d)

    def e_br(n):
        p = piece_b(order[n], -1)
        copies.arrive(("br", n), "bx", p)
        if n % 2 == 0:
            copies.send(("bf", n), "bf", p, p, right)
        share_b(order[n], -1)

    def e_bl(n):
        p = piece_b(order[n], 1)
        copies.arrive(("bl", n), "bx", p)
        if n % 2 == 1:
            copies.send(("bf", n), "bf", p, p, left_x)
        share_b(order[n], 1)

    def e_bf(n):
        copies.arrive(("bf", n), "bf", piece_b(order[n], 2))
        share_b(order[n], 2)

    def e_proj(n):
        zz = zi(z + order[n])
        copies.arrive(("sa", n), "sa", full_a.at[zz, :, 1 - core])
        copies.arrive(("sb", n), "sb", full_b.at[zz, :, 1 - core])
        blk = rows_full[zz].reshape(tokens, width)
        part_a = dot(blk, full_a[zz].reshape(width, full_a.shape[4]))
        part_b = dot(blk, full_b[zz, :, :, :, : inner + PAD].reshape(width, inner + PAD))
        if n == 0:
            acc_a[...] = part_a
            acc_b[...] = part_b
        else:
            acc_a[...] += part_a
            acc_b[...] += part_b

    def e_table(o):
        base = ((me - o + groups) % groups) * per_dev
        seen = jnp.int32(0)
        pages = [jnp.int32(0)] * CAP
        for q in range(per_dev):
            hit = owner_dev[base + q] == me
            page = jnp.where(hit, state_page[base + q], -1)
            conv = jnp.where(hit, conv_page[base + q], -1)
            kept = accepted[base + q]
            info = (o * CAP + seen) + conv * 64 + kept * 1024
            back = page + kept * 1024
            for p in range(per_dev):
                by_page[p] = jnp.where(page == p, info, by_page[p])
                by_conv[p] = jnp.where(conv == p, back, by_conv[p])
            for c in range(CAP):
                pages[c] = jnp.where(hit & (seen == c), page, pages[c])
            seen = seen + hit.astype(jnp.int32)
        for c in range(CAP):
            table[8 + o * CAP + c] = pages[c]

    by_page = [jnp.int32(0)] * per_dev
    by_conv = [jnp.int32(0)] * per_dev

    def e_rows():
        for o in range(1, WINDOW):
            copies.arrive(("h", o), "h", incoming.at[pl.ds(o * CAP, CAP)])
        for p in range(per_dev):
            table[24 + p] = jnp.minimum(by_page[p] & 63, SLOTS - 1)
            table[32 + p] = jnp.minimum((by_page[p] >> 6) & 15, per_dev - 1)
            table[40 + p] = jnp.minimum(by_page[p] >> 10, draft)
            table[48 + p] = jnp.minimum(by_conv[p] & 1023, per_dev - 1)
            table[56 + p] = jnp.minimum(by_conv[p] >> 10, draft)
        for p in range(per_dev):
            rows_full[col, p] = incoming[table[24 + p]]
        for k in range(1, mdl_size):
            copies.send(("y", k), "y", rows_full.at[col], rows_full.at[col], across[k - 1])

    def e_rows_in():
        for k in range(1, mdl_size):
            copies.arrive(("y", k), "y", rows_full.at[(col - k + mdl_size) % mdl_size])

    for o in range(1, WINDOW):
        part = pl.ds(o * CAP, CAP)
        copies.send(("h", o), "h", outgoing.at[part], incoming.at[part], ahead[o - 1])
    incoming[0:CAP] = outgoing[0:CAP]

    own_a, own_b = piece_a(0, 0), piece_b(0, 0)
    b_up(1)
    b_down(1)
    for d in range(1, XN):
        copies.send(("ax", d), "ax", own_a, own_a, xs[d - 1])
    a_up(1, 0)
    a_down(1, 0)
    b_side(0)
    share_a(0, 0)
    share_b(0, 0)


    run = {
        "ax": e_ax,
        "bu": e_bu,
        "bd": e_bd,
        "bz": e_bz,
        "au": e_au,
        "ad": e_ad,
        "br": e_br,
        "bl": e_bl,
        "bf": e_bf,
        "proj": e_proj,
    }
    for o in range(WINDOW):
        e_table(o)
    lead = 8 - (KCONV - 1)

    def e_state(p):
        state_low[p] = state[p].reshape(inner, nstate).astype(bf16)

    def e_history():
        hist_x[...] = hist_inner[...].astype(f32)
        hist_s[...] = hist_state[...].astype(f32)
        for p in range(per_dev):
            for j in range(KCONV - 1):
                series_x[p, lead + j : lead + j + 1, :] = hist_x[j, pl.ds(table[32 + p], 1), :]
                series_s[p, lead + j : lead + j + 1, :] = hist_s[j, pl.ds(table[32 + p], 1), :]

    started, projected = False, False
    for n, event in enumerate(ORDER):
        if event[0] == "au" and not started:
            started = True
            e_rows()
        if event[0] == "proj" and not projected:
            projected = True
            e_rows_in()
        run[event[0]](*event[1:])
        if n == 11:
            load_state.wait()
        if 12 <= n < 12 + 2 * per_dev and n % 2 == 0:
            e_state((n - 12) // 2)
        if n == 13:
            e_history()

    series_x[:, 8:, :] = acc_b[:, :inner].astype(bf16).astype(f32).reshape(per_dev, draft, inner)
    series_s[:, 8:, :] = (
        acc_a[:, inner:].astype(bf16).astype(f32).reshape(per_dev, draft, 2 * nstate)
    )

    def conv(series, taps):
        total = taps[0:1, :] * series[:, lead : lead + draft, :]
        for k in range(1, KCONV):
            total = total + taps[k : k + 1, :] * series[:, lead + k : lead + k + draft, :]
        return jax.nn.silu(total).reshape(tokens, total.shape[2])

    active = conv(series_x, conv_inner)
    maps = conv(series_s, conv_state)
    b_rows, c_rows = maps[:, :nstate], maps[:, nstate:]

    lane = lax.broadcasted_iota(jnp.int32, (1, PAD), 1)
    bias_row = jnp.zeros((1, PAD), f32)
    rate_row = jnp.zeros((1, PAD), f32)
    for h in range(heads):
        bias_row = jnp.where(lane == h, step_bias[h], bias_row)
        rate_row = jnp.where(lane == h, decay_log[h], rate_row)
    rate_row = jnp.exp(rate_row)
    step_raw = acc_b[:, inner:].astype(bf16).astype(f32)
    size = jax.nn.softplus(step_raw + bias_row)
    rows_i = lax.broadcasted_iota(jnp.int32, (tokens, tokens), 0)
    cols_i = lax.broadcasted_iota(jnp.int32, (tokens, tokens), 1)
    causal = (rows_i // draft == cols_i // draft) & (cols_i <= rows_i)
    decay = dot(causal.astype(f32), -size * rate_row, HIGH)
    decay_t, size_t = decay.T, size.T
    scores = dot_nt(c_rows, b_rows, HIGH)
    end_at = jnp.zeros((tokens, tokens), jnp.int32)
    for p in range(per_dev):
        end_at = jnp.where(rows_i // draft == p, p * draft + table[40 + p] - 1, end_at)
    end_decay = dot((cols_i == end_at).astype(f32), decay, HIGH)
    before = rows_i <= end_at
    chosen_w = jnp.where(before, jnp.exp(jnp.where(before, end_decay - decay, 0.0)), 0.0) * size
    grown = jnp.exp(decay)
    decay_s[...] = jnp.exp(end_decay)

    b_low = b_rows.astype(bf16)
    c_low = c_rows.astype(bf16)
    c_rest = (c_rows - c_low.astype(f32)).astype(bf16)
    for p in range(per_dev):
        mine = slice(p * draft, (p + 1) * draft)
        both = jnp.concatenate([c_low[mine], c_rest[mine]], axis=0)
        found = dot_nt(both, state_low[p])
        carried[mine, :] = found[:draft] + found[draft:]

    left = lax.broadcasted_iota(jnp.int32, (tokens, PAD), 1) < hdim

    def spread(values, j):
        return jnp.where(left, values[:, 2 * j : 2 * j + 1], values[:, 2 * j + 1 : 2 * j + 2])

    total = jnp.zeros((tokens, PAD), f32)
    gated_cols = []
    for j in range(heads // 2):
        cols = slice(j * PAD, (j + 1) * PAD)
        x_pair = active[:, cols]
        x_low = x_pair.astype(bf16)
        x_rest = (x_pair - x_low.astype(f32)).astype(bf16)
        pair = []
        for h in (2 * j, 2 * j + 1):
            gap = decay[:, h : h + 1] - decay_t[h : h + 1, :]
            weight = jnp.exp(jnp.where(causal, gap, -1e30)) * scores * size_t[h : h + 1, :]
            w_low = weight.astype(bf16)
            w_rest = (weight - w_low.astype(f32)).astype(bf16)
            pair.append(dot(w_low, x_low) + dot(w_rest, x_low) + dot(w_low, x_rest))
        skip = jnp.where(left, skip_gain[2 * j], skip_gain[2 * j + 1])
        y = (
            jnp.where(left, pair[0], pair[1])
            + carried[:, cols] * spread(grown, j)
            + skip * x_pair
        )
        gated = y.astype(bf16).astype(f32) * jax.nn.silu(acc_a[:, cols])
        total = total + gated * gated
        gated_cols.append((gated * norm_gain[0:1, cols]).astype(bf16))
    gated_low = jnp.concatenate(gated_cols, axis=1)
    squares[...] = dot_nt(jnp.ones((8, PAD), f32), total, HIGH)
    for k in range(1, mdl_size):
        copies.send(("s", k), "s", squares, square_parts.at[k], across[k - 1])

    def project_out(k):
        m = (col + k + mdl_size) % mdl_size
        block = full_b[m, :, :, :, inner + PAD :].reshape(columns, inner)
        return dot_nt(gated_low, block)

    def ring(k):
        return across[k % mdl_size - 1]

    low, high = pl.ds(0, tokens // 2), pl.ds(tokens // 2, tokens // 2)
    terms[4] = project_out(4).astype(bf16)
    copies.send(("t4u",), "t", terms.at[4, low], parts.at[2, low], ring(2))
    copies.send(("t4d",), "t", terms.at[4, high], parts.at[2, high], ring(-2))
    for k, name, slot in ((3, "t3u", 0), (-3, "t3d", 1), (1, "t1u", 3), (-1, "t1d", 4)):
        terms[k % mdl_size] = project_out(k).astype(bf16)
        towards = 1 if k > 0 else -1
        copies.send((name,), "t", terms.at[k % mdl_size], parts.at[slot], ring(towards))
    sums[0] = project_out(2)
    sums[1] = project_out(-2)
    own_term = project_out(0)

    picked_t = []
    for j in range(heads // 2):
        cols = slice(j * PAD, (j + 1) * PAD)
        picked_t.append((active[:, cols] * spread(chosen_w, j)).T.astype(bf16))
    picked = jnp.concatenate(picked_t, axis=0)
    row_of = lax.broadcasted_iota(jnp.int32, (tokens, nstate), 0) // draft
    stores = []
    for p in range(per_dev):
        added = dot(picked, jnp.where(row_of == p, b_low, jnp.zeros_like(b_low)))
        for h in range(heads):
            factor = decay_s[p * draft : p * draft + 1, h : h + 1]
            state[p, h] = factor * state[p, h] + added[h * hdim : (h + 1) * hdim, :]
        store = pltpu.make_async_copy(state.at[p], new_states.at[p], local_sem.at[2 + p])
        store.start()
        stores.append(store)
    copies.arrive(("t3u",), "t", parts.at[0])
    copies.arrive(("t4u",), "t", parts.at[2, low])
    sums[0] += parts[0].astype(f32)
    sums[0, low, :] += parts[2, low, :].astype(f32)
    terms[2] = sums[0].astype(bf16)
    copies.send(("t2u",), "t", terms.at[2], parts.at[5], ring(2))
    copies.arrive(("t3d",), "t", parts.at[1])
    copies.arrive(("t4d",), "t", parts.at[2, high])
    sums[1] += parts[1].astype(f32)
    sums[1, high, :] += parts[2, high, :].astype(f32)
    terms[mdl_size - 2] = sums[1].astype(bf16)
    copies.send(("t2d",), "t", terms.at[mdl_size - 2], parts.at[6], ring(-2))
    for c in range(per_dev):
        for j in range(KCONV - 1):
            row = pl.ds(lead + table[56 + c] + j, 1)
            edge_x[j, c : c + 1, :] = series_x[table[48 + c], row, :]
            edge_s[j, c : c + 1, :] = series_s[table[48 + c], row, :]
    edge_inner[...] = edge_x[...].astype(bf16)
    edge_state[...] = edge_s[...].astype(bf16)

    square_parts[0] = squares[...]
    for k in range(1, mdl_size):
        copies.arrive(("s", k), "s", square_parts.at[k])
    stacked = square_parts[...].reshape(mdl_size * 8, tokens)
    eighth = jnp.full((mdl_size * 8, columns), 0.125, f32)
    mean = lax.dot_general(
        stacked, eighth, TN, preferred_element_type=f32, precision=HIGH
    ) / (mdl_size * inner)
    scale = lax.rsqrt(mean + EPSILON)
    for name, slot in (("t1u", 3), ("t1d", 4), ("t2u", 5), ("t2d", 6)):
        copies.arrive((name,), "t", parts.at[slot])
        own_term = own_term + parts[slot].astype(f32)
    result[...] = (own_term * scale).astype(bf16).reshape(per_dev, draft, columns)
    for s in range(SLOTS):
        outgoing2[s] = result[table[8 + s]]
    for o in range(1, WINDOW):
        part = pl.ds(o * CAP, CAP)
        copies.send(("r", o), "r", outgoing2.at[part], incoming2.at[part], behind[o - 1])
    incoming2[0:CAP] = outgoing2[0:CAP]

    copies.sent("a", full_a.at[pl.ds(0, half - 1)])
    copies.sent("a_last", full_a.at[0, pl.ds(0, 2)])
    copies.sent("ax", full_a.at[0, pl.ds(0, XN - 1), 0])
    copies.sent("b", full_b.at[0, pl.ds(0, half - 1)])
    copies.sent("b_last", full_b.at[0, 0, 0])
    copies.sent("bx", full_b.at[pl.ds(0, 2)])
    copies.sent("bf", full_b.at[0])
    copies.sent("sa", full_a.at[pl.ds(0, half)])
    copies.sent("sb", full_b.at[pl.ds(0, half)])
    copies.sent("h", incoming.at[pl.ds(CAP, SLOTS - CAP)])
    copies.sent("y", rows_full.at[pl.ds(1, mdl_size - 1)])
    copies.sent("s", square_parts.at[pl.ds(1, mdl_size - 1)])
    copies.sent("t", parts.at[pl.ds(1, mdl_size - 1)])
    for store in stores:
        store.wait()
    for o in range(1, WINDOW):
        copies.arrive(("r", o), "r", incoming2.at[pl.ds(o * CAP, CAP)])
    for q in range(per_dev):
        mixed[q] = incoming2[table[q]]
    copies.sent("r", incoming2.at[pl.ds(CAP, SLOTS - CAP)])


def store_kernel(mixed, states, edge_inner, edge_state, *refs):
    outs, held, sems = refs[:4], refs[4:8], refs[8]
    parts = [(states.at[p], outs[1].at[p], held[1].at[p]) for p in range(states.shape[0])]
    for source, out, hold in (
        (mixed, outs[0], held[0]),
        (edge_inner, outs[2], held[2]),
        (edge_state, outs[3], held[3]),
    ):
        parts.append((source, out, hold))
    loads = [
        pltpu.make_async_copy(source, hold, sems.at[0, i])
        for i, (source, _, hold) in enumerate(parts)
    ]
    stores = [
        pltpu.make_async_copy(hold, out, sems.at[1, i]) for i, (_, out, hold) in enumerate(parts)
    ]
    for load in loads:
        load.start()
    for load, store in zip(loads, stores, strict=True):
        load.wait()
        store.start()
    for store in stores:
        store.wait()


def store(*arrays):
    hbm = pl.BlockSpec(memory_space=pl.ANY)
    return pl.pallas_call(
        store_kernel,
        out_shape=tuple(jax.ShapeDtypeStruct(a.shape, a.dtype) for a in arrays),
        in_specs=[hbm] * 4,
        out_specs=(hbm,) * 4,
        scratch_shapes=[pltpu.VMEM(a.shape, a.dtype) for a in arrays]
        + [pltpu.SemaphoreType.DMA((2, arrays[1].shape[0] + 3))],
        compiler_params=pltpu.CompilerParams(vmem_limit_bytes=60 << 20),
        name="store_results",
    )(*arrays)


def on_device(
    hidden_in,
    z_weight,
    x_weight,
    state_proj,
    step_weight,
    step_bias,
    decay_log,
    skip_gain,
    conv_inner,
    conv_state,
    norm_gain,
    out_weight,
    state_pool,
    conv_pool_inner,
    conv_pool_state,
    owner_dev,
    state_page,
    conv_page,
    accepted,
):
    groups = lax.axis_size("req")
    mdl_size = lax.axis_size("mdl")
    per_dev, heads, hdim, nstate = state_pool.shape
    tokens, depth = hidden_in.shape
    draft = tokens // per_dev
    inner = heads * hdim
    zn = groups // (2 * XN)
    rows = z_weight.shape[0]
    width = depth // mdl_size
    columns = depth // mdl_size
    f32, bf16 = jnp.float32, jnp.bfloat16
    smem = pl.BlockSpec(memory_space=pltpu.SMEM)
    vmem = pl.BlockSpec(memory_space=pltpu.VMEM)
    hbm = pl.BlockSpec(memory_space=pl.ANY)
    hist_inner = conv_pool_inner.transpose(1, 0, 2)
    hist_state = conv_pool_state.transpose(1, 0, 2)
    edge = (KCONV - 1, per_dev)
    mixed, new_states, edge_inner, edge_state = pl.pallas_call(
        functools.partial(layer_kernel, groups, mdl_size),
        out_shape=(
            jax.ShapeDtypeStruct((per_dev, draft, columns), bf16),
            jax.ShapeDtypeStruct(state_pool.shape, state_pool.dtype),
            jax.ShapeDtypeStruct(hist_inner.shape, hist_inner.dtype),
            jax.ShapeDtypeStruct(hist_state.shape, hist_state.dtype),
        ),
        in_specs=[smem] * 7 + [vmem] * 10 + [hbm] * 2,
        out_specs=(vmem, hbm, vmem, vmem),
        scratch_shapes=[
            pltpu.VMEM((zn, XN, 2, rows, inner + 2 * nstate), bf16),
            pltpu.VMEM((zn, XN, 2, rows, 2 * inner + PAD), bf16),
            pltpu.VMEM((mdl_size, per_dev, draft, width), bf16),
            pltpu.VMEM((per_dev, draft, width), bf16),
            pltpu.VMEM((SLOTS, draft, width), bf16),
            pltpu.VMEM((SLOTS, draft, width), bf16),
            pltpu.VMEM(state_pool.shape, f32),
            pltpu.VMEM((per_dev, inner, nstate), bf16),
            pltpu.VMEM((tokens, inner + 2 * nstate), f32),
            pltpu.VMEM((tokens, inner + PAD), f32),
            pltpu.VMEM((per_dev, draft + 8, inner), f32),
            pltpu.VMEM((per_dev, draft + 8, 2 * nstate), f32),
            pltpu.VMEM(edge + (inner,), f32),
            pltpu.VMEM(edge + (2 * nstate,), f32),
            pltpu.VMEM(edge + (inner,), f32),
            pltpu.VMEM(edge + (2 * nstate,), f32),
            pltpu.VMEM((tokens, inner), f32),
            pltpu.SMEM((64,), jnp.int32),
            pltpu.VMEM((tokens, PAD), f32),
            pltpu.VMEM((mdl_size, tokens, columns), bf16),
            pltpu.VMEM((2, tokens, columns), f32),
            pltpu.VMEM((8, tokens), f32),
            pltpu.VMEM((mdl_size, tokens, columns), bf16),
            pltpu.VMEM((mdl_size, 8, tokens), f32),
            pltpu.VMEM((per_dev, draft, columns), bf16),
            pltpu.VMEM((SLOTS, draft, columns), bf16),
            pltpu.VMEM((SLOTS, draft, columns), bf16),
            pltpu.SemaphoreType.DMA((16,)),
            pltpu.SemaphoreType.DMA((120,)),
            pltpu.SemaphoreType.DMA((2 + per_dev,)),
        ],
        compiler_params=pltpu.CompilerParams(
            collective_id=0, has_side_effects=True, vmem_limit_bytes=58 << 20
        ),
        name="draft_layer",
    )(
        owner_dev,
        state_page,
        conv_page,
        accepted,
        step_bias,
        decay_log,
        skip_gain,
        z_weight,
        x_weight,
        state_proj,
        step_weight.T,
        out_weight.T,
        conv_inner,
        conv_state,
        norm_gain.reshape(1, -1),
        hist_inner,
        hist_state,
        hidden_in.reshape(per_dev, draft, depth),
        state_pool,
    )
    mixed, new_states, edge_inner, edge_state = store(
        mixed, new_states, edge_inner, edge_state
    )
    return (
        mixed.reshape(tokens, columns),
        new_states,
        edge_inner.transpose(1, 0, 2),
        edge_state.transpose(1, 0, 2),
    )


def solution(mesh):
    return jax.shard_map(
        on_device,
        mesh=mesh,
        in_specs=(
            P("req", None),
            P("req", "mdl"),
            P("req", "mdl"),
            P("req", None),
            P("req", "mdl"),
            P("mdl"),
            P("mdl"),
            P("mdl"),
            P(None, "mdl"),
            P(),
            P("mdl"),
            P("mdl", "req"),
            P("req", "mdl", None, None),
            P("req", None, "mdl"),
            P("req", None, None),
            P(),
            P(),
            P(),
            P(),
        ),
        out_specs=(
            P("req", "mdl"),
            P("req", "mdl", None, None),
            P("req", None, "mdl"),
            P("req", None, None),
        ),
        check_vma=False,
    )
```

```python
import functools

import jax
import jax.numpy as jnp
from jax import lax
from jax.experimental import pallas as pl
from jax.experimental.pallas import tpu as pltpu
from jax.sharding import PartitionSpec as P

KCONV = 4
CAP = 2
WINDOW = 8
SLOTS = WINDOW * CAP
XN = 4
PAD = 128
HIGH = lax.Precision.HIGHEST
EPSILON = 1e-05

ORDER = (
    ("ax", 1), ("ax", 3), ("bu", 1), ("bd", 1), ("ax", 2), ("au", 1, 0), ("ad", 1, 0), ("bl", 0),
    ("au", 1, 1), ("ad", 1, 1), ("br", 0), ("bl", 1), ("au", 1, 3), ("ad", 1, 3), ("br", 1),
    ("bl", 2), ("bu", 2), ("bd", 2), ("br", 2), ("au", 1, 2), ("ad", 1, 2), ("bf", 1),
    ("au", 2, 0), ("ad", 2, 0), ("bf", 0), ("bl", 3), ("au", 2, 1), ("ad", 2, 1), ("br", 3),
    ("au", 2, 3), ("ad", 2, 3), ("bl", 4), ("br", 4), ("bu", 3), ("bd", 3), ("bf", 3),
    ("au", 2, 2), ("ad", 2, 2), ("bf", 2), ("au", 3, 0), ("ad", 3, 0), ("bf", 4), ("bl", 5),
    ("au", 3, 1), ("ad", 3, 1), ("proj", 0), ("proj", 1), ("au", 3, 3), ("ad", 3, 3), ("br", 5),
    ("bl", 6), ("proj", 2), ("bz", 4), ("proj", 3), ("br", 6), ("bf", 5), ("au", 3, 2),
    ("ad", 3, 2), ("proj", 4), ("au", 4, 0), ("ad", 4, 3), ("proj", 5), ("br", 7), ("bl", 7),
    ("au", 4, 1), ("ad", 4, 2), ("bf", 6), ("bf", 7), ("proj", 6), ("proj", 7),
)
MESH = pl.DeviceIdType.MESH
NT = (((1,), (1,)), ((), ()))
TN = (((0,), (0,)), ((), ()))


def dot(a, b, precision=None):
    return jnp.dot(a, b, preferred_element_type=jnp.float32, precision=precision)


def dot_nt(a, b, precision=None):
    return lax.dot_general(a, b, NT, preferred_element_type=jnp.float32, precision=precision)


class Copies:
    def __init__(self, send_sem, recv_sem, anyone):
        self.send_sem, self.recv_sem, self.anyone = send_sem, recv_sem, anyone
        self.keys, self.groups = {}, {}

    def describe(self, name, group, src, dst, peer):
        k = self.keys.setdefault(name, len(self.keys))
        g = self.groups.setdefault(group, len(self.groups))
        return pltpu.make_async_remote_copy(
            src_ref=src,
            dst_ref=dst,
            send_sem=self.send_sem.at[g],
            recv_sem=self.recv_sem.at[k],
            device_id=peer,
            device_id_type=MESH,
        )

    def send(self, name, group, src, dst, peer):
        self.describe(name, group, src, dst, peer).start()

    def arrive(self, name, group, where):
        self.describe(name, group, where, where, self.anyone).wait_recv()

    def sent(self, group, whole):
        pltpu.make_async_copy(whole, whole, self.send_sem.at[self.groups[group]]).wait()


def layer_kernel(
    groups,
    mdl_size,
    owner_dev,
    state_page,
    conv_page,
    accepted,
    step_bias,
    decay_log,
    skip_gain,
    z_weight,
    x_weight,
    state_proj,
    step_t,
    out_t,
    conv_inner,
    conv_state,
    norm_gain,
    hist_inner,
    hist_state,
    hidden,
    state_pool,
    mixed,
    new_states,
    edge_inner,
    edge_state,
    full_a,
    full_b,
    rows_full,
    slice_in,
    outgoing,
    incoming,
    state,
    state_low,
    acc_a,
    acc_b,
    series_x,
    series_s,
    hist_x,
    hist_s,
    edge_x,
    edge_s,
    carried,
    table,
    decay_s,
    terms,
    sums,
    squares,
    parts,
    square_parts,
    result,
    outgoing2,
    incoming2,
    send_sem,
    recv_sem,
    local_sem,
):
    f32, bf16 = jnp.float32, jnp.bfloat16
    per_dev, draft, columns = mixed.shape
    tokens = per_dev * draft
    heads, hdim, nstate = state.shape[1:]
    inner = heads * hdim
    width = slice_in.shape[2]
    zn = groups // (2 * XN)
    me = lax.axis_index("req")
    col = lax.axis_index("mdl")
    core = me % 2
    x = (me // 2) % XN
    z = me // (2 * XN)

    def zi(v):
        return (v + zn) % zn

    def xi(v):
        return (v + XN) % XN

    def at(zz, xx):
        return {"req": (zi(zz) * XN + xi(xx)) * 2 + core}

    load_rows = pltpu.make_async_copy(
        hidden.at[:, :, pl.ds(pl.multiple_of(col * width, width), width)],
        slice_in,
        local_sem.at[0],
    )
    load_rows.start()
    load_state = pltpu.make_async_copy(state_pool, state, local_sem.at[1])
    load_state.start()

    sibling = {"req": me + 1 - 2 * core}
    up, down = at(z + 1, x), at(z - 1, x)
    right, left_x = at(z, x + 1), at(z, x - 1)
    xs = [at(z, x + d) for d in range(1, XN)]
    ahead = [{"req": (me + o) % groups} for o in range(1, WINDOW)]
    behind = [{"req": (me - o + groups) % groups} for o in range(1, WINDOW)]
    across = [{"mdl": (col + k) % mdl_size} for k in range(1, mdl_size)]
    peers = [sibling, up, down] + xs + ahead + behind + across
    barrier = pltpu.get_barrier_semaphore()
    for peer in peers:
        pl.semaphore_signal(barrier, inc=1, device_id=peer, device_id_type=MESH)

    full_a[z, x, core, :, :inner] = z_weight[...]
    full_a[z, x, core, :, inner:] = state_proj[...]
    full_b[z, x, core, :, :inner] = x_weight[...]
    place = (
        lax.broadcasted_iota(jnp.int32, (heads, PAD), 0)
        == lax.broadcasted_iota(jnp.int32, (heads, PAD), 1)
    ).astype(f32)
    full_b[z, x, core, :, inner : inner + PAD] = lax.dot_general(
        step_t[...].astype(f32), place, TN, preferred_element_type=f32, precision=HIGH
    ).astype(bf16)
    full_b[z, x, core, :, inner + PAD :] = out_t[...]
    owners = [owner_dev[me * per_dev + q] for q in range(per_dev)]
    slots = []
    for q in range(per_dev):
        offset = owners[q] - me
        offset = jnp.where(offset < 0, offset + groups, offset)
        rank = jnp.int32(0)
        for r in range(q):
            rank = rank + (owners[r] == owners[q]).astype(jnp.int32)
        slots.append(offset * CAP + rank)
        table[q] = jnp.minimum(slots[q], SLOTS - 1)
    load_rows.wait()
    for s in range(SLOTS):
        source = jnp.int32(0)
        for q in range(per_dev):
            source = jnp.where(slots[q] == s, q, source)
        outgoing[s] = slice_in[source]
    pl.semaphore_wait(barrier, len(peers))

    copies = Copies(send_sem, recv_sem, up)
    half = zn // 2
    rows = full_a.shape[3]
    halves = (pl.ds(0, rows // 2), pl.ds(rows // 2, rows // 2))
    order = [0]
    for s in range(1, half):
        order += [-s, s]
    order.append(-half)
    place_of = {d: n for n, d in enumerate(order)}

    def piece_a(dz, dx):
        return full_a.at[zi(z + dz), xi(x + dx), core]

    def piece_b(dz, dx):
        return full_b.at[zi(z + dz), xi(x + dx), core]

    def share_a(dz, dx):
        p = piece_a(dz, dx)
        copies.send(("sa", place_of[dz]), "sa", p, p, sibling)

    def share_b(dz, dx):
        p = piece_b(dz, dx)
        copies.send(("sb", place_of[dz]), "sb", p, p, sibling)

    def a_up(s, d):
        group = "a_last" if s == half else "a"
        copies.send(("au", s, d), group, piece_a(1 - s, -d), piece_a(1 - s, -d), up)

    def a_down(s, d):
        group = "a_last" if s == half else "a"
        copies.send(("ad", s, d), group, piece_a(s - 1, -d), piece_a(s - 1, -d), down)

    up_last, down_last = range(0, XN // 2), range(XN // 2, XN)

    def b_up(s):
        p = piece_b(1 - s, 0)
        if s == half:
            copies.send(("bu", s), "b_last", p.at[halves[0]], p.at[halves[0]], up)
        else:
            copies.send(("bu", s), "b", p, p, up)

    def b_down(s):
        p = piece_b(s - 1, 0)
        if s == half:
            copies.send(("bd", s), "b_last", p.at[halves[1]], p.at[halves[1]], down)
        else:
            copies.send(("bd", s), "b", p, p, down)

    def b_side(n):
        p = piece_b(order[n], 0)
        copies.send(("br", n), "bx", p, p, right)
        copies.send(("bl", n), "bx", p, p, left_x)

    def e_ax(d):
        copies.arrive(("ax", d), "ax", piece_a(0, -d))
        a_up(1, d)
        a_down(1, d)
        share_a(0, -d)

    def e_bu(s):
        copies.arrive(("bu", s), "b", piece_b(-s, 0))
        b_up(s + 1)
        b_side(place_of[-s])
        share_b(-s, 0)

    def e_bd(s):
        copies.arrive(("bd", s), "b", piece_b(s, 0))
        b_down(s + 1)
        b_side(place_of[s])
        share_b(s, 0)

    def e_bz(s):
        copies.arrive(("bu", s), "b_last", piece_b(-s, 0).at[halves[0]])
        copies.arrive(("bd", s), "b_last", piece_b(-s, 0).at[halves[1]])
        b_side(place_of[-s])
        share_b(-s, 0)

    def e_au(s, d):
        copies.arrive(("au", s, d), "a" if s < half else "a_last", piece_a(-s, -d))
        if s + 1 < half or (s < half and d in up_last):
            a_up(s + 1, d)
        share_a(-s, -d)

    def e_ad(s, d):
        copies.arrive(("ad", s, d), "a" if s < half else "a_last", piece_a(s, -d))
        if s + 1 < half or (s < half and d in down_last):
            a_down(s + 1, d)
        share_a(s if s < half else -s, -d)

    def e_br(n):
        p = piece_b(order[n], -1)
        copies.arrive(("br", n), "bx", p)
        if n % 2 == 0:
            copies.send(("bf", n), "bf", p, p, right)
        share_b(order[n], -1)

    def e_bl(n):
        p = piece_b(order[n], 1)
        copies.arrive(("bl", n), "bx", p)
        if n % 2 == 1:
            copies.send(("bf", n), "bf", p, p, left_x)
        share_b(order[n], 1)

    def e_bf(n):
        copies.arrive(("bf", n), "bf", piece_b(order[n], 2))
        share_b(order[n], 2)

    def e_proj(n):
        zz = zi(z + order[n])
        copies.arrive(("sa", n), "sa", full_a.at[zz, :, 1 - core])
        copies.arrive(("sb", n), "sb", full_b.at[zz, :, 1 - core])
        blk = rows_full[zz].reshape(tokens, width)
        part_a = dot(blk, full_a[zz].reshape(width, full_a.shape[4]))
        part_b = dot(blk, full_b[zz, :, :, :, : inner + PAD].reshape(width, inner + PAD))
        if n == 0:
            acc_a[...] = part_a
            acc_b[...] = part_b
        else:
            acc_a[...] += part_a
            acc_b[...] += part_b

    def e_table(o):
        base = ((me - o + groups) % groups) * per_dev
        seen = jnp.int32(0)
        pages = [jnp.int32(0)] * CAP
        for q in range(per_dev):
            hit = owner_dev[base + q] == me
            page = jnp.where(hit, state_page[base + q], -1)
            conv = jnp.where(hit, conv_page[base + q], -1)
            kept = accepted[base + q]
            info = (o * CAP + seen) + conv * 64 + kept * 1024
            back = page + kept * 1024
            for p in range(per_dev):
                by_page[p] = jnp.where(page == p, info, by_page[p])
                by_conv[p] = jnp.where(conv == p, back, by_conv[p])
            for c in range(CAP):
                pages[c] = jnp.where(hit & (seen == c), page, pages[c])
            seen = seen + hit.astype(jnp.int32)
        for c in range(CAP):
            table[8 + o * CAP + c] = pages[c]

    by_page = [jnp.int32(0)] * per_dev
    by_conv = [jnp.int32(0)] * per_dev

    def e_rows():
        for o in range(1, WINDOW):
            copies.arrive(("h", o), "h", incoming.at[pl.ds(o * CAP, CAP)])
        for p in range(per_dev):
            table[24 + p] = jnp.minimum(by_page[p] & 63, SLOTS - 1)
            table[32 + p] = jnp.minimum((by_page[p] >> 6) & 15, per_dev - 1)
            table[40 + p] = jnp.minimum(by_page[p] >> 10, draft)
            table[48 + p] = jnp.minimum(by_conv[p] & 1023, per_dev - 1)
            table[56 + p] = jnp.minimum(by_conv[p] >> 10, draft)
        for p in range(per_dev):
            rows_full[col, p] = incoming[table[24 + p]]
        for k in range(1, mdl_size):
            copies.send(("y", k), "y", rows_full.at[col], rows_full.at[col], across[k - 1])

    def e_rows_in():
        for k in range(1, mdl_size):
            copies.arrive(("y", k), "y", rows_full.at[(col - k + mdl_size) % mdl_size])

    for o in range(1, WINDOW):
        part = pl.ds(o * CAP, CAP)
        copies.send(("h", o), "h", outgoing.at[part], incoming.at[part], ahead[o - 1])
    incoming[0:CAP] = outgoing[0:CAP]

    own_a, own_b = piece_a(0, 0), piece_b(0, 0)
    b_up(1)
    b_down(1)
    for d in range(1, XN):
        copies.send(("ax", d), "ax", own_a, own_a, xs[d - 1])
    a_up(1, 0)
    a_down(1, 0)
    b_side(0)
    share_a(0, 0)
    share_b(0, 0)


    run = {
        "ax": e_ax,
        "bu": e_bu,
        "bd": e_bd,
        "bz": e_bz,
        "au": e_au,
        "ad": e_ad,
        "br": e_br,
        "bl": e_bl,
        "bf": e_bf,
        "proj": e_proj,
    }
    for o in range(WINDOW):
        e_table(o)
    lead = 8 - (KCONV - 1)

    def e_state(p):
        state_low[p] = state[p].reshape(inner, nstate).astype(bf16)

    def e_history():
        hist_x[...] = hist_inner[...].astype(f32)
        hist_s[...] = hist_state[...].astype(f32)
        for p in range(per_dev):
            for j in range(KCONV - 1):
                series_x[p, lead + j : lead + j + 1, :] = hist_x[j, pl.ds(table[32 + p], 1), :]
                series_s[p, lead + j : lead + j + 1, :] = hist_s[j, pl.ds(table[32 + p], 1), :]

    started, projected = False, False
    for n, event in enumerate(ORDER):
        if event[0] == "au" and not started:
            started = True
            e_rows()
        if event[0] == "proj" and not projected:
            projected = True
            e_rows_in()
        run[event[0]](*event[1:])
        if n == 11:
            load_state.wait()
        if 12 <= n < 12 + 2 * per_dev and n % 2 == 0:
            e_state((n - 12) // 2)
        if n == 13:
            e_history()

    series_x[:, 8:, :] = acc_b[:, :inner].astype(bf16).astype(f32).reshape(per_dev, draft, inner)
    series_s[:, 8:, :] = (
        acc_a[:, inner:].astype(bf16).astype(f32).reshape(per_dev, draft, 2 * nstate)
    )

    def conv(series, taps):
        total = taps[0:1, :] * series[:, lead : lead + draft, :]
        for k in range(1, KCONV):
            total = total + taps[k : k + 1, :] * series[:, lead + k : lead + k + draft, :]
        return jax.nn.silu(total).reshape(tokens, total.shape[2])

    active = conv(series_x, conv_inner)
    maps = conv(series_s, conv_state)
    b_rows, c_rows = maps[:, :nstate], maps[:, nstate:]

    lane = lax.broadcasted_iota(jnp.int32, (1, PAD), 1)
    bias_row = jnp.zeros((1, PAD), f32)
    rate_row = jnp.zeros((1, PAD), f32)
    for h in range(heads):
        bias_row = jnp.where(lane == h, step_bias[h], bias_row)
        rate_row = jnp.where(lane == h, decay_log[h], rate_row)
    rate_row = jnp.exp(rate_row)
    step_raw = acc_b[:, inner:].astype(bf16).astype(f32)
    size = jax.nn.softplus(step_raw + bias_row)
    rows_i = lax.broadcasted_iota(jnp.int32, (tokens, tokens), 0)
    cols_i = lax.broadcasted_iota(jnp.int32, (tokens, tokens), 1)
    causal = (rows_i // draft == cols_i // draft) & (cols_i <= rows_i)
    decay = dot(causal.astype(f32), -size * rate_row, HIGH)
    decay_t, size_t = decay.T, size.T
    scores = dot_nt(c_rows, b_rows, HIGH)
    end_at = jnp.zeros((tokens, tokens), jnp.int32)
    for p in range(per_dev):
        end_at = jnp.where(rows_i // draft == p, p * draft + table[40 + p] - 1, end_at)
    end_decay = dot((cols_i == end_at).astype(f32), decay, HIGH)
    before = rows_i <= end_at
    chosen_w = jnp.where(before, jnp.exp(jnp.where(before, end_decay - decay, 0.0)), 0.0) * size
    grown = jnp.exp(decay)
    decay_s[...] = jnp.exp(end_decay)

    b_low = b_rows.astype(bf16)
    c_low = c_rows.astype(bf16)
    c_rest = (c_rows - c_low.astype(f32)).astype(bf16)
    for p in range(per_dev):
        mine = slice(p * draft, (p + 1) * draft)
        both = jnp.concatenate([c_low[mine], c_rest[mine]], axis=0)
        found = dot_nt(both, state_low[p])
        carried[mine, :] = found[:draft] + found[draft:]

    left = lax.broadcasted_iota(jnp.int32, (tokens, PAD), 1) < hdim

    def spread(values, j):
        return jnp.where(left, values[:, 2 * j : 2 * j + 1], values[:, 2 * j + 1 : 2 * j + 2])

    total = jnp.zeros((tokens, PAD), f32)
    gated_cols = []
    for j in range(heads // 2):
        cols = slice(j * PAD, (j + 1) * PAD)
        x_pair = active[:, cols]
        x_low = x_pair.astype(bf16)
        x_rest = (x_pair - x_low.astype(f32)).astype(bf16)
        pair = []
        for h in (2 * j, 2 * j + 1):
            gap = decay[:, h : h + 1] - decay_t[h : h + 1, :]
            weight = jnp.exp(jnp.where(causal, gap, -1e30)) * scores * size_t[h : h + 1, :]
            w_low = weight.astype(bf16)
            w_rest = (weight - w_low.astype(f32)).astype(bf16)
            pair.append(dot(w_low, x_low) + dot(w_rest, x_low) + dot(w_low, x_rest))
        skip = jnp.where(left, skip_gain[2 * j], skip_gain[2 * j + 1])
        y = (
            jnp.where(left, pair[0], pair[1])
            + carried[:, cols] * spread(grown, j)
            + skip * x_pair
        )
        gated = y.astype(bf16).astype(f32) * jax.nn.silu(acc_a[:, cols])
        total = total + gated * gated
        gated_cols.append((gated * norm_gain[0:1, cols]).astype(bf16))
    gated_low = jnp.concatenate(gated_cols, axis=1)

    def project_out(k):
        m = (col + k + mdl_size) % mdl_size
        block = full_b[m, :, :, :, inner + PAD :].reshape(columns, inner)
        return dot_nt(gated_low, block)

    def ring(k):
        return across[k % mdl_size - 1]

    low, high = pl.ds(0, tokens // 2), pl.ds(tokens // 2, tokens // 2)
    terms[4] = project_out(4).astype(bf16)
    copies.send(("t4u",), "t", terms.at[4, low], parts.at[2, low], ring(2))
    copies.send(("t4d",), "t", terms.at[4, high], parts.at[2, high], ring(-2))
    for k, name, slot in ((3, "t3u", 0), (-3, "t3d", 1), (1, "t1u", 3), (-1, "t1d", 4)):
        terms[k % mdl_size] = project_out(k).astype(bf16)
        towards = 1 if k > 0 else -1
        copies.send((name,), "t", terms.at[k % mdl_size], parts.at[slot], ring(towards))
    squares[...] = dot_nt(jnp.ones((8, PAD), f32), total, HIGH)
    for k in range(1, mdl_size):
        copies.send(("s", k), "s", squares, square_parts.at[k], across[k - 1])
    sums[0] = project_out(2)
    sums[1] = project_out(-2)
    own_term = project_out(0)

    picked_t = []
    for j in range(heads // 2):
        cols = slice(j * PAD, (j + 1) * PAD)
        picked_t.append((active[:, cols] * spread(chosen_w, j)).T.astype(bf16))
    picked = jnp.concatenate(picked_t, axis=0)
    row_of = lax.broadcasted_iota(jnp.int32, (tokens, nstate), 0) // draft
    stores = []
    for p in range(per_dev):
        added = dot(picked, jnp.where(row_of == p, b_low, jnp.zeros_like(b_low)))
        for h in range(heads):
            factor = decay_s[p * draft : p * draft + 1, h : h + 1]
            state[p, h] = factor * state[p, h] + added[h * hdim : (h + 1) * hdim, :]
        store = pltpu.make_async_copy(state.at[p], new_states.at[p], local_sem.at[2 + p])
        store.start()
        stores.append(store)
    copies.arrive(("t3u",), "t", parts.at[0])
    copies.arrive(("t4u",), "t", parts.at[2, low])
    sums[0] += parts[0].astype(f32)
    sums[0, low, :] += parts[2, low, :].astype(f32)
    terms[2] = sums[0].astype(bf16)
    copies.send(("t2u",), "t", terms.at[2], parts.at[5], ring(2))
    copies.arrive(("t3d",), "t", parts.at[1])
    copies.arrive(("t4d",), "t", parts.at[2, high])
    sums[1] += parts[1].astype(f32)
    sums[1, high, :] += parts[2, high, :].astype(f32)
    terms[mdl_size - 2] = sums[1].astype(bf16)
    copies.send(("t2d",), "t", terms.at[mdl_size - 2], parts.at[6], ring(-2))
    for c in range(per_dev):
        for j in range(KCONV - 1):
            row = pl.ds(lead + table[56 + c] + j, 1)
            edge_x[j, c : c + 1, :] = series_x[table[48 + c], row, :]
            edge_s[j, c : c + 1, :] = series_s[table[48 + c], row, :]
    edge_inner[...] = edge_x[...].astype(bf16)
    edge_state[...] = edge_s[...].astype(bf16)

    square_parts[0] = squares[...]
    for k in range(1, mdl_size):
        copies.arrive(("s", k), "s", square_parts.at[k])
    stacked = square_parts[...].reshape(mdl_size * 8, tokens)
    eighth = jnp.full((mdl_size * 8, columns), 0.125, f32)
    mean = lax.dot_general(
        stacked, eighth, TN, preferred_element_type=f32, precision=HIGH
    ) / (mdl_size * inner)
    scale = lax.rsqrt(mean + EPSILON)
    for name, slot in (("t1u", 3), ("t1d", 4), ("t2u", 5), ("t2d", 6)):
        copies.arrive((name,), "t", parts.at[slot])
        own_term = own_term + parts[slot].astype(f32)
    result[...] = (own_term * scale).astype(bf16).reshape(per_dev, draft, columns)
    for s in range(SLOTS):
        outgoing2[s] = result[table[8 + s]]
    for o in range(1, WINDOW):
        part = pl.ds(o * CAP, CAP)
        copies.send(("r", o), "r", outgoing2.at[part], incoming2.at[part], behind[o - 1])
    incoming2[0:CAP] = outgoing2[0:CAP]

    copies.sent("a", full_a.at[pl.ds(0, half - 1)])
    copies.sent("a_last", full_a.at[0, pl.ds(0, 2)])
    copies.sent("ax", full_a.at[0, pl.ds(0, XN - 1), 0])
    copies.sent("b", full_b.at[0, pl.ds(0, half - 1)])
    copies.sent("b_last", full_b.at[0, 0, 0])
    copies.sent("bx", full_b.at[pl.ds(0, 2)])
    copies.sent("bf", full_b.at[0])
    copies.sent("sa", full_a.at[pl.ds(0, half)])
    copies.sent("sb", full_b.at[pl.ds(0, half)])
    copies.sent("h", incoming.at[pl.ds(CAP, SLOTS - CAP)])
    copies.sent("y", rows_full.at[pl.ds(1, mdl_size - 1)])
    copies.sent("s", square_parts.at[pl.ds(1, mdl_size - 1)])
    copies.sent("t", parts.at[pl.ds(1, mdl_size - 1)])
    for store in stores:
        store.wait()
    for o in range(1, WINDOW):
        copies.arrive(("r", o), "r", incoming2.at[pl.ds(o * CAP, CAP)])
    for q in range(per_dev):
        mixed[q] = incoming2[table[q]]
    copies.sent("r", incoming2.at[pl.ds(CAP, SLOTS - CAP)])


def store_kernel(mixed, states, edge_inner, edge_state, *refs):
    outs, held, sems = refs[:4], refs[4:8], refs[8]
    parts = [(states.at[p], outs[1].at[p], held[1].at[p]) for p in range(states.shape[0])]
    for source, out, hold in (
        (mixed, outs[0], held[0]),
        (edge_inner, outs[2], held[2]),
        (edge_state, outs[3], held[3]),
    ):
        parts.append((source, out, hold))
    loads = [
        pltpu.make_async_copy(source, hold, sems.at[0, i])
        for i, (source, _, hold) in enumerate(parts)
    ]
    stores = [
        pltpu.make_async_copy(hold, out, sems.at[1, i]) for i, (_, out, hold) in enumerate(parts)
    ]
    for load in loads:
        load.start()
    for load, store in zip(loads, stores, strict=True):
        load.wait()
        store.start()
    for store in stores:
        store.wait()


def store(*arrays):
    hbm = pl.BlockSpec(memory_space=pl.ANY)
    return pl.pallas_call(
        store_kernel,
        out_shape=tuple(jax.ShapeDtypeStruct(a.shape, a.dtype) for a in arrays),
        in_specs=[hbm] * 4,
        out_specs=(hbm,) * 4,
        scratch_shapes=[pltpu.VMEM(a.shape, a.dtype) for a in arrays]
        + [pltpu.SemaphoreType.DMA((2, arrays[1].shape[0] + 3))],
        compiler_params=pltpu.CompilerParams(vmem_limit_bytes=60 << 20),
        name="store_results",
    )(*arrays)


def on_device(
    hidden_in,
    z_weight,
    x_weight,
    state_proj,
    step_weight,
    step_bias,
    decay_log,
    skip_gain,
    conv_inner,
    conv_state,
    norm_gain,
    out_weight,
    state_pool,
    conv_pool_inner,
    conv_pool_state,
    owner_dev,
    state_page,
    conv_page,
    accepted,
):
    groups = lax.axis_size("req")
    mdl_size = lax.axis_size("mdl")
    per_dev, heads, hdim, nstate = state_pool.shape
    tokens, depth = hidden_in.shape
    draft = tokens // per_dev
    inner = heads * hdim
    zn = groups // (2 * XN)
    rows = z_weight.shape[0]
    width = depth // mdl_size
    columns = depth // mdl_size
    f32, bf16 = jnp.float32, jnp.bfloat16
    smem = pl.BlockSpec(memory_space=pltpu.SMEM)
    vmem = pl.BlockSpec(memory_space=pltpu.VMEM)
    hbm = pl.BlockSpec(memory_space=pl.ANY)
    hist_inner = conv_pool_inner.transpose(1, 0, 2)
    hist_state = conv_pool_state.transpose(1, 0, 2)
    edge = (KCONV - 1, per_dev)
    mixed, new_states, edge_inner, edge_state = pl.pallas_call(
        functools.partial(layer_kernel, groups, mdl_size),
        out_shape=(
            jax.ShapeDtypeStruct((per_dev, draft, columns), bf16),
            jax.ShapeDtypeStruct(state_pool.shape, state_pool.dtype),
            jax.ShapeDtypeStruct(hist_inner.shape, hist_inner.dtype),
            jax.ShapeDtypeStruct(hist_state.shape, hist_state.dtype),
        ),
        in_specs=[smem] * 7 + [vmem] * 10 + [hbm] * 2,
        out_specs=(vmem, hbm, vmem, vmem),
        scratch_shapes=[
            pltpu.VMEM((zn, XN, 2, rows, inner + 2 * nstate), bf16),
            pltpu.VMEM((zn, XN, 2, rows, 2 * inner + PAD), bf16),
            pltpu.VMEM((mdl_size, per_dev, draft, width), bf16),
            pltpu.VMEM((per_dev, draft, width), bf16),
            pltpu.VMEM((SLOTS, draft, width), bf16),
            pltpu.VMEM((SLOTS, draft, width), bf16),
            pltpu.VMEM(state_pool.shape, f32),
            pltpu.VMEM((per_dev, inner, nstate), bf16),
            pltpu.VMEM((tokens, inner + 2 * nstate), f32),
            pltpu.VMEM((tokens, inner + PAD), f32),
            pltpu.VMEM((per_dev, draft + 8, inner), f32),
            pltpu.VMEM((per_dev, draft + 8, 2 * nstate), f32),
            pltpu.VMEM(edge + (inner,), f32),
            pltpu.VMEM(edge + (2 * nstate,), f32),
            pltpu.VMEM(edge + (inner,), f32),
            pltpu.VMEM(edge + (2 * nstate,), f32),
            pltpu.VMEM((tokens, inner), f32),
            pltpu.SMEM((64,), jnp.int32),
            pltpu.VMEM((tokens, PAD), f32),
            pltpu.VMEM((mdl_size, tokens, columns), bf16),
            pltpu.VMEM((2, tokens, columns), f32),
            pltpu.VMEM((8, tokens), f32),
            pltpu.VMEM((mdl_size, tokens, columns), bf16),
            pltpu.VMEM((mdl_size, 8, tokens), f32),
            pltpu.VMEM((per_dev, draft, columns), bf16),
            pltpu.VMEM((SLOTS, draft, columns), bf16),
            pltpu.VMEM((SLOTS, draft, columns), bf16),
            pltpu.SemaphoreType.DMA((16,)),
            pltpu.SemaphoreType.DMA((120,)),
            pltpu.SemaphoreType.DMA((2 + per_dev,)),
        ],
        compiler_params=pltpu.CompilerParams(
            collective_id=0, has_side_effects=True, vmem_limit_bytes=58 << 20
        ),
        name="draft_layer",
    )(
        owner_dev,
        state_page,
        conv_page,
        accepted,
        step_bias,
        decay_log,
        skip_gain,
        z_weight,
        x_weight,
        state_proj,
        step_weight.T,
        out_weight.T,
        conv_inner,
        conv_state,
        norm_gain.reshape(1, -1),
        hist_inner,
        hist_state,
        hidden_in.reshape(per_dev, draft, depth),
        state_pool,
    )
    mixed, new_states, edge_inner, edge_state = store(
        mixed, new_states, edge_inner, edge_state
    )
    return (
        mixed.reshape(tokens, columns),
        new_states,
        edge_inner.transpose(1, 0, 2),
        edge_state.transpose(1, 0, 2),
    )


def solution(mesh):
    return jax.shard_map(
        on_device,
        mesh=mesh,
        in_specs=(
            P("req", None),
            P("req", "mdl"),
            P("req", "mdl"),
            P("req", None),
            P("req", "mdl"),
            P("mdl"),
            P("mdl"),
            P("mdl"),
            P(None, "mdl"),
            P(),
            P("mdl"),
            P("mdl", "req"),
            P("req", "mdl", None, None),
            P("req", None, "mdl"),
            P("req", None, None),
            P(),
            P(),
            P(),
            P(),
        ),
        out_specs=(
            P("req", "mdl"),
            P("req", "mdl", None, None),
            P("req", None, "mdl"),
            P("req", None, None),
        ),
        check_vma=False,
    )
```
